32 devices in a mesh: table: 8 (over z, x), replica: 4 (over y, core).
Axes of the slice: x: 2, y: 2, z: 4, core: 2. Of those that a mesh axis runs over, the one named last changes fastest.
Arguments:
- emb_table: bfloat16 [8192, 128], P('table'), may hold values from -3 to 3
- cross_up: bfloat16 [256, 3456], replicated, may hold values from -0.375 to 0.375
- cross_down: bfloat16 [256, 3456], replicated, may hold values from -0.109375 to 0.109375
- cross_bias: float32 [3456], replicated, may hold values from -3 to 3
- out_weight: float32 [3456], replicated, may hold values from -0.109375 to 0.109375
- bottom_weight: float32 [13, 128], replicated, may hold values from -1.75 to 1.75
- bottom_bias: float32 [128], replicated, may hold values from -3 to 3
- dense_in: float32 [4096, 13], P(('table', 'replica')), may hold values from -6 to 6
- labels: int32 [4096], P(('table', 'replica')), may hold values from 0 to 1
- lookup_ids: int32 [4096, 26, 4], P(('table', 'replica')), may hold values from 0 to 767
- bag_weight: float32 [4096, 26, 4], P(('table', 'replica')), may hold values from 0.25 to 1
- bag_length: int32 [4096, 26], P(('table', 'replica')), may hold values from 1 to 4
- want_blocks: int32 [8, 4, 8, 1], P('table', 'replica'), may hold values from 0 to 31
- hot_blocks: int32 [8, 2], P('table'), may hold values from 0 to 31
- hot_count: int32 [8], P('table'), may hold values from 1 to 2, as said below
Outputs:
- up_grad: float32 [256, 3456], P(('table', 'replica'))
- down_grad: float32 [256, 3456], P(('table', 'replica'))
- table_grad: float32 [8192, 128], P(('table', 'replica'))
The draws below stay inside these ranges and needn't reach their ends.
Inputs may be any that keep to these rules, and one draw needn't show every extreme that they name: `hot_count`: each owner has 1 to 2 live hot slots, and some owner has 2.
All inputs are finite; a program needn't handle non-finite values.
Results may differ from the reference program's by a relative error of at most 0.0053.
Values may be sent and summed in bfloat16 or wider, within the bound.
A program may use at most 64 MiB of HBM per device.

```python
import jax
import jax.numpy as jnp
from jax import lax

EMB = 128
FEATS = 26
DENSE = 13
RANK = 256
BLOCK = 32
BAG = 4
WANT = 1
HOT_MOST = 2
B_DEV = 128
BLOCKS_DEV = 32
OWNERS = 8
ROWS = 8192
CACHE = 768
DI = 3456
SAMPLES = 4096
N_TABLE = 8
N_REPLICA = 4


def draw_hot_count(key, part):
    first_key, second_key = jax.random.split(jax.random.fold_in(key, 7))
    doubled = (jax.random.randint(first_key, (OWNERS,), 0, 4) == 0).astype(jnp.int32) * (HOT_MOST - 1)
    chosen = jax.random.randint(second_key, (), 0, OWNERS)
    return jnp.where(jnp.arange(OWNERS) == chosen, HOT_MOST, 1 + doubled).astype(jnp.int32)


def with_ends(entries, rng, least, high):
    longest = entries.shape.index(max(entries.shape))
    spots = []
    for shift in (0, 1):
        where = [jax.random.randint(jax.random.fold_in(rng, axis), (), 0, length) for axis, length in enumerate(entries.shape)]
        where[longest] = (where[longest] + shift) % entries.shape[longest]
        spots.append(tuple(where))
    return entries.at[spots[0]].set(least).at[spots[1]].set(high)


def shard_levels(own_key, dims, cuts, low, largest):
    gain = 1.0
    for axis_at, shards_of in cuts:
        steps = jax.random.uniform(jax.random.fold_in(jax.random.fold_in(own_key, 6), axis_at), (shards_of,), jnp.float32, low / len(cuts), largest / len(cuts))
        gain = gain * jnp.repeat(jnp.exp(steps), dims[axis_at] // shards_of).reshape((-1,) + (1,) * (len(dims) - 1 - axis_at))
    return gain


def gaussian(rng, shape, scale, bound, pieces=(), kind=jnp.bfloat16):
    result = scale * jax.random.normal(rng, shape, jnp.float32)
    if pieces:
        result = result * shard_levels(rng, shape, pieces, -0.22, 0.18)
    return jnp.clip(result, -bound, bound).astype(kind)


def setup_inputs(seed: int = 0) -> dict:
    streams_of = jax.random.split(jax.random.key(seed), 16)
    return {
        "emb_table": gaussian(streams_of[0], (ROWS, EMB), 0.5, 3.0, ((0, 8),)),
        "cross_up": gaussian(streams_of[1], (RANK, DI), RANK ** -0.5, 0.375),
        "cross_down": gaussian(streams_of[2], (RANK, DI), DI ** -0.5, 0.109375),
        "cross_bias": gaussian(streams_of[3], (DI,), 0.5, 3.0, (), jnp.float32),
        "out_weight": gaussian(streams_of[4], (DI,), DI ** -0.5, 0.109375, (), jnp.float32),
        "bottom_weight": gaussian(streams_of[5], (DENSE, EMB), DENSE ** -0.5, 1.75, (), jnp.float32),
        "bottom_bias": gaussian(streams_of[6], (EMB,), 0.5, 3.0, (), jnp.float32),
        "dense_in": gaussian(streams_of[7], (SAMPLES, DENSE), 1.0, 6.0, ((0, 32),), jnp.float32),
        "labels": with_ends(jax.random.randint(streams_of[8], (SAMPLES,), 0, 2), jax.random.fold_in(streams_of[8], 1), 0, 1).astype(jnp.int32),
        "lookup_ids": with_ends(jax.random.randint(streams_of[9], (SAMPLES, FEATS, BAG), 0, CACHE), jax.random.fold_in(streams_of[9], 1), 0, CACHE - 1).astype(jnp.int32),
        "bag_weight": jnp.clip(0.25 + 0.75 * jax.random.uniform(streams_of[10], (SAMPLES, FEATS, BAG), jnp.float32) ** shard_levels(streams_of[10], (SAMPLES, FEATS, BAG), ((0, 32),), -0.2, 0.2), 0.25, 1.0),
        "bag_length": with_ends(jax.random.randint(streams_of[11], (SAMPLES, FEATS), 1, BAG + 1), jax.random.fold_in(streams_of[11], 1), 1, BAG).astype(jnp.int32),
        "want_blocks": with_ends(jax.random.randint(streams_of[12], (OWNERS, N_REPLICA, OWNERS, WANT), 0, BLOCKS_DEV), jax.random.fold_in(streams_of[12], 1), 0, BLOCKS_DEV - 1).astype(jnp.int32),
        "hot_blocks": with_ends(jax.random.randint(streams_of[13], (OWNERS, HOT_MOST), 0, BLOCKS_DEV), jax.random.fold_in(streams_of[13], 1), 0, BLOCKS_DEV - 1).astype(jnp.int32),
        "hot_count": draw_hot_count(jax.random.fold_in(streams_of[15], 71), 0),
    }


def local_step(cached_rows, dense_dev, labels_dev, ids_dev, weight_dev, length_dev, cross_up, cross_down, cross_bias, out_weight, bottom_weight, bottom_bias):
    batch = ids_dev.shape[0]
    width = cached_rows.shape[1]
    gathered = cached_rows[ids_dev].astype(jnp.float32)
    slots = jnp.arange(ids_dev.shape[2], dtype=jnp.int32)
    bag_coef = jnp.where(slots[None, None, :] < length_dev[:, :, None], weight_dev, jnp.zeros((), jnp.float32))
    pooled = jnp.sum(bag_coef[..., None] * gathered, axis=2)
    bottom = jax.nn.relu(jnp.dot(dense_dev, bottom_weight, precision=lax.Precision.HIGHEST) + bottom_bias)
    cross_base = jnp.concatenate([bottom, pooled.reshape(batch, -1)], 1).astype(jnp.bfloat16)
    low_rank = lax.dot_general(cross_base, cross_down, (((1,), (1,)), ((), ())), preferred_element_type=jnp.float32).astype(jnp.bfloat16)
    cross_gate = jnp.dot(low_rank, cross_up, preferred_element_type=jnp.float32) + cross_bias
    base_wide = cross_base.astype(jnp.float32)
    crossed = base_wide * cross_gate + base_wide
    logits = jnp.dot(crossed, out_weight, precision=lax.Precision.HIGHEST)
    logit_grad = jax.nn.sigmoid(logits) - labels_dev.astype(jnp.float32)
    grad_crossed = logit_grad[:, None] * out_weight[None, :]
    g_cross = (grad_crossed * base_wide).astype(jnp.bfloat16)
    g_low = lax.dot_general(g_cross, cross_up, (((1,), (1,)), ((), ())), preferred_element_type=jnp.float32).astype(jnp.bfloat16)
    up_part = lax.dot_general(low_rank, g_cross, (((0,), (0,)), ((), ())), preferred_element_type=jnp.float32)
    down_part = lax.dot_general(g_low, cross_base, (((0,), (0,)), ((), ())), preferred_element_type=jnp.float32)
    grad_base = grad_crossed * (cross_gate + 1.0) + jnp.dot(g_low, cross_down, preferred_element_type=jnp.float32)
    grad_pooled = grad_base[:, width:].reshape(batch, -1, width)
    contrib = bag_coef[..., None] * grad_pooled[:, :, None, :]
    cache_grad = jnp.zeros(cached_rows.shape, jnp.float32).at[ids_dev.reshape(-1)].add(contrib.reshape(-1, width))
    return up_part, down_part, cache_grad


def reference(emb_table, cross_up, cross_down, cross_bias, out_weight, bottom_weight, bottom_bias, dense_in, labels, lookup_ids, bag_weight, bag_length, want_blocks, hot_blocks, hot_count):
    devices_all = N_TABLE * N_REPLICA
    blocks = emb_table.reshape(OWNERS, BLOCKS_DEV, BLOCK, EMB)
    owner_ids = jnp.arange(OWNERS, dtype=jnp.int32)
    alive = jnp.arange(HOT_MOST, dtype=jnp.int32)[:, None] < hot_count[None, :]
    hot_rows = jnp.where(alive[:, :, None, None], blocks[owner_ids[None, :], hot_blocks.T], jnp.zeros((), jnp.bfloat16))
    hot_flat = hot_rows.reshape(-1, EMB)
    cold_count = OWNERS * WANT * BLOCK
    wanted = want_blocks.reshape(devices_all, OWNERS, WANT)
    items = (wanted,
             dense_in.reshape(devices_all, B_DEV, DENSE),
             labels.reshape(devices_all, B_DEV),
             lookup_ids.reshape(devices_all, B_DEV, FEATS, BAG),
             bag_weight.reshape(devices_all, B_DEV, FEATS, BAG),
             bag_length.reshape(devices_all, B_DEV, FEATS))

    def device_turn(running, device_item):
        block_grad, hot_grad, up_sum, down_sum = running
        wanted_dev, dense_dev, labels_dev, ids_dev, weight_dev, length_dev = device_item
        cold_rows = blocks[owner_ids[:, None], wanted_dev]
        cached_rows = jnp.concatenate([cold_rows.reshape(-1, EMB), hot_flat], 0)
        up_part, down_part, cache_grad = local_step(cached_rows, dense_dev, labels_dev, ids_dev, weight_dev, length_dev, cross_up, cross_down, cross_bias, out_weight, bottom_weight, bottom_bias)
        cold_grad = lax.optimization_barrier(cache_grad[:cold_count].astype(jnp.bfloat16)).astype(jnp.float32)
        block_grad = block_grad.at[owner_ids[:, None], wanted_dev].add(cold_grad.reshape(OWNERS, WANT, BLOCK, EMB))
        hot_grad = hot_grad + cache_grad[cold_count:]
        return (block_grad, hot_grad, up_sum + up_part, down_sum + down_part), None

    start = (jnp.zeros((OWNERS, BLOCKS_DEV, BLOCK, EMB), jnp.float32),
             jnp.zeros((HOT_MOST * OWNERS * BLOCK, EMB), jnp.float32),
             jnp.zeros((RANK, DI), jnp.float32),
             jnp.zeros((RANK, DI), jnp.float32))
    (block_grad, hot_grad, up_sum, down_sum), _ = lax.scan(device_turn, start, items)
    hot_sums = jnp.where(alive[:, :, None, None], hot_grad.reshape(HOT_MOST, OWNERS, BLOCK, EMB), jnp.zeros((), jnp.float32))
    block_grad = block_grad.at[owner_ids[None, :], hot_blocks.T].add(hot_sums)
    return up_sum, down_sum, block_grad.reshape(ROWS, EMB)
```

```python
import functools

import jax
import jax.numpy as jnp
from jax import lax
from jax.experimental import pallas as pl
from jax.experimental.pallas import tpu as pltpu
from jax.sharding import PartitionSpec as P

EMB = 128
BLOCK = 32
LANES = 128
SUBLANES = 8
MESH = pl.DeviceIdType.MESH
CHUNKS = 3
PARTS = 9
EARLY = 0
F32 = jnp.float32
BF16 = jnp.bfloat16


def vmem(n):
    return [pl.BlockSpec(memory_space=pltpu.VMEM)] * n


def pick_rows(ids, emb_ref):
    total = emb_ref.shape[0]
    tiles = total // LANES
    row = lax.broadcasted_iota(jnp.int32, (BLOCK, LANES), 0)
    lane = lax.broadcasted_iota(jnp.int32, (BLOCK, LANES), 1)
    parts = []
    for block in ids:
        want = block * BLOCK + row
        parts.append(
            jnp.concatenate(
                [jnp.where(want == lane + LANES * c, 1.0, 0.0) for c in range(tiles)], axis=1
            )
        )
    pick = jnp.concatenate(parts, axis=0).astype(BF16)
    return jnp.dot(pick, emb_ref[...], preferred_element_type=F32).astype(BF16)


def whole_kernel(
    plan, stages, n_table, n_rep, buffers,
    want_ref, hot_ids_ref, count_ref, emb_hbm, ids_hbm, weight_hbm, length_hbm, dense_hbm,
    label_hbm, up_hbm, down_hbm, bias_hbm, outw_hbm, bw_hbm, bb_hbm,
    up_out, down_out, table_out,
    emb_ref, ids_ref, weight_ref, length_ref, dense_ref, label_ref, up_ref, down_ref,
    bias_ref, outw_ref, bw_ref, bb_ref, want_v, ask, serve, own_hot, cold_in, hot_in,
    pick, pick_low, base, part_sum, bow, grad_t, ids_cols, coef_cols, turn,
    x_own, x_send, x_in, acc, acc_hot, hot_send, hot_recv, tg_cold, ag_cold, ag_hot, ag_ids,
    *rest,
):
    sends = rest[:buffers]
    recvs = rest[buffers:2 * buffers]
    (load_sem, id_send, id_recv, hs_send, hs_recv, cs_send, cs_recv, b_send, b_recv,
     w_send, w_recv, c_send, c_recv, a_send, a_recv, i_send, i_recv, g_send, g_recv,
     m_send, m_recv) = rest[2 * buffers:]
    t = lax.axis_index("table")
    r = lax.axis_index("replica")
    wants = serve.shape[1]
    slots = own_hot.shape[0]
    feats, batch, cache = pick.shape
    bag = ids_ref.shape[1]
    width = base.shape[1]
    group = 16
    core = lax.rem(r, 2)
    mate = (t, r + 1 - 2 * core)

    def table_peer(k):
        return (lax.rem(t + k, n_table), r)

    def rep_peer(k):
        return (t, lax.rem(r + k, n_rep))

    def remote(src, dst, send, recv, device):
        return pltpu.make_async_remote_copy(
            src_ref=src, dst_ref=dst, send_sem=send, recv_sem=recv,
            device_id=device, device_id_type=MESH,
        )

    barrier = pltpu.get_barrier_semaphore()
    for k in range(1, n_table):
        pl.semaphore_signal(barrier, inc=1, device_id=table_peer(k), device_id_type=MESH)
    for k in range(1, n_rep):
        pl.semaphore_signal(barrier, inc=1, device_id=rep_peer(k), device_id_type=MESH)
    loads = [
        pltpu.make_async_copy(src, dst, load_sem.at[i])
        for i, (src, dst) in enumerate((
            (emb_hbm, emb_ref), (ids_hbm, ids_ref), (weight_hbm, weight_ref),
            (length_hbm, length_ref), (dense_hbm, dense_ref), (label_hbm, label_ref),
            (bw_hbm, bw_ref), (bb_hbm, bb_ref), (bias_hbm, bias_ref), (outw_hbm, outw_ref),
            (down_hbm, down_ref), (up_hbm, up_ref),
        ))
    ]
    for c in loads:
        c.start()
    for p in range(n_table):
        for w in range(wants):
            want_v[p, w:w + 1] = jnp.full((1, LANES), want_ref[0, 0, w, p], jnp.int32)
    ask[t] = want_v[t]
    hot_rows = []
    for s in range(slots):
        block = jnp.where(s < count_ref[0], hot_ids_ref[0, s], -1)
        hot_rows.append(jnp.full((1, LANES), block, jnp.int32))
    loads[0].wait()
    hot = pick_rows(hot_rows, emb_ref).reshape(slots, BLOCK, EMB)
    own_hot[...] = hot
    half_block = pl.ds(pl.multiple_of(core * (BLOCK // 2), BLOCK // 2), BLOCK // 2)
    hot_in[:, t, half_block] = own_hot[:, half_block]
    for c in loads[1:10]:
        c.wait()
    turn[...] = jnp.zeros_like(turn)
    for f in range(feats):
        turn[f * bag:(f + 1) * bag, :] = ids_ref[f].astype(F32)
    ids_cols[...] = turn[...].T
    spot = lax.broadcasted_iota(jnp.int32, (bag, batch), 0)
    for f in range(feats):
        live = spot < length_ref[f:f + 1, :]
        turn[f * bag:(f + 1) * bag, :] = jnp.where(live, weight_ref[f], 0.0)
    coef_cols[...] = turn[...].T

    def build(first, last):
        @pl.loop(first, last)
        def _(g):
            at = pl.ds(pl.multiple_of(g * group, group), group)
            ids = ids_cols[at, :]
            coef = coef_cols[at, :]
            lane = lax.broadcasted_iota(jnp.int32, (group, cache), 1).astype(F32)
            for f in range(feats):
                total = None
                for l in range(bag):
                    j = f * bag + l
                    term = jnp.where(ids[:, j:j + 1] == lane, coef[:, j:j + 1], 0.0)
                    total = term if total is None else total + term
                high = total.astype(BF16)
                pick[f, at, :] = high
                pick_low[f, at, :] = (total - high.astype(F32)).astype(BF16)

    build(0, EARLY)
    pl.semaphore_wait(barrier, n_table - 1 + n_rep - 1)

    id_copies = [
        remote(want_v.at[table_peer(k)[0]], ask.at[t], id_send.at[k], id_recv.at[k], table_peer(k))
        for k in range(1, n_table)
    ]
    hot_copies = [
        remote(own_hot.at[:, half_block], hot_in.at[:, t, half_block], hs_send.at[k],
               hs_recv.at[k], table_peer(k))
        for k in range(1, n_table)
    ]
    for c in id_copies + hot_copies:
        c.start()

    groups = batch // group
    first = groups * 5 // 8
    build(EARLY, first)
    for c in id_copies:
        c.wait()
    asked = [ask[p, w:w + 1, :] for p in range(n_table) for w in range(wants)]
    serve[...] = pick_rows(asked, emb_ref).reshape(n_table, wants, BLOCK, EMB)
    cold_copies = [
        remote(serve.at[table_peer(k)[0]], cold_in.at[t], cs_send.at[k], cs_recv.at[k],
               table_peer(k))
        for k in range(1, n_table)
    ]
    for c in cold_copies:
        c.start()
    for c in hot_copies:
        c.wait()
    hot_mate = remote(
        hot_in.at[:, :, half_block], hot_in.at[:, :, half_block], m_send.at[0], m_recv.at[0], mate
    )
    hot_mate.start()
    cold_in[t] = serve[t]
    ag_ids[r] = ask[...]
    id_shares = [
        remote(ask, ag_ids.at[r], i_send.at[k], i_recv.at[k], rep_peer(k)) for k in range(1, n_rep)
    ]
    for c in id_shares:
        c.start()
    build(first, groups)

    bottom = jnp.zeros((batch, EMB), F32) + bb_ref[...]
    features = dense_ref.shape[0]
    turn[0:features, :] = dense_ref[...]
    turn[features:features + 1, :] = label_ref[...].astype(F32)
    dense = turn[...].T
    label = dense[:, features:features + 1]
    for j in range(features):
        bottom = bottom + dense[:, j:j + 1] * bw_ref[j:j + 1, :]
    lsum = jnp.zeros((batch, LANES), F32)

    def settle(lsum, j, value):
        cols = slice(j * EMB, (j + 1) * EMB)
        b = value.astype(BF16)
        base[0:batch, cols] = b
        x = b.astype(F32) * outw_ref[cols].reshape(1, -1)
        bow[:, cols] = x.astype(BF16)
        return lsum + x * (bias_ref[cols].reshape(1, -1) + 1.0)

    lsum = settle(lsum, 0, jnp.maximum(bottom, 0.0))
    cold = n_table * wants * BLOCK
    some = 2 if feats % 2 == 0 else 1

    def pool(f, cols, rows):
        at = slice(f, f + some)
        return jnp.dot(
            pick[at, :, cols].reshape(some * batch, -1), rows, preferred_element_type=F32
        ) + jnp.dot(
            pick_low[at, :, cols].reshape(some * batch, -1), rows, preferred_element_type=F32
        )

    hot_mate.wait()
    rows = hot_in[...].reshape(cache - cold, EMB)
    for f in range(0, feats, some):
        pooled = pool(f, slice(cold, cache), rows)
        for i in range(some):
            part_sum[:, (f + i) * EMB:(f + i + 1) * EMB] = pooled[i * batch:(i + 1) * batch]
    for c in cold_copies:
        c.wait()
    rows = cold_in[...].reshape(cold, EMB)
    wide = width // CHUNKS
    base_copies = []
    for f in range(0, feats, some):
        pooled = pool(f, slice(0, cold), rows)
        for i in range(some):
            before = part_sum[:, (f + i) * EMB:(f + i + 1) * EMB]
            lsum = settle(lsum, f + i + 1, pooled[i * batch:(i + 1) * batch] + before)
        n = len(base_copies)
        while n < CHUNKS and (f + some + 1) * EMB >= (n + 1) * wide:
            cols = slice(n * wide, (n + 1) * wide)
            base_copies.append(remote(
                base.at[0:batch, cols], base.at[batch:2 * batch, cols], b_send.at[n],
                b_recv.at[n], mate,
            ))
            base_copies[n].start()
            n += 1

    nt = (((1,), (1,)), ((), ()))
    for c in loads[10:]:
        c.wait()
    low = lax.dot_general(base[0:batch], down_ref[...], nt, preferred_element_type=F32)
    high = lax.dot_general(bow[...], up_ref[...], nt, preferred_element_type=F32)
    low_b = low.astype(BF16)
    prod = low_b.astype(F32) * high
    rank = prod.shape[1]
    for i in range(rank // LANES):
        lsum = lsum + prod[:, i * LANES:(i + 1) * LANES]
    logit = jnp.sum(lsum, axis=1, keepdims=True)
    lgrad = jax.nn.sigmoid(logit) - label
    g_low_f = high * lgrad
    g_low = g_low_f.astype(BF16)
    chips, two = acc.shape[0], acc.shape[1]
    own = two // 2
    turned = jnp.concatenate([low * lgrad, g_low_f], axis=1).T
    turned = turned.reshape(2, chips, 2, own, batch)
    is_first = core == 0
    mine = jnp.where(is_first, turned[:, :, 0], turned[:, :, 1])
    other = jnp.where(is_first, turned[:, :, 1], turned[:, :, 0])
    x_send[...] = other.reshape(rank, batch).astype(BF16)
    x_copy = remote(x_send, x_in, m_send.at[1], m_recv.at[1], mate)
    x_copy.start()
    x_own[...] = mine.reshape(rank, batch).astype(BF16)

    def bit_of(axis, bit):
        return lax.rem((t if axis == "table" else r) // (1 << bit), 2)

    def partner(axis, bit):
        shift = (1 - 2 * bit_of(axis, bit)) * (1 << bit)
        return (t + shift, r) if axis == "table" else (t, r + shift)

    parts = len(plan) - 1
    step = width // parts
    lows = [0] * (parts + 1)
    sizes = [chips] * (parts + 1)
    copies = {}
    deep = len(stages[0])

    def sums(p):
        return (acc, slice(p * step, (p + 1) * step)) if p < parts else (acc_hot, slice(0, EMB))

    def launch(p, s):
        axis, bit = stages[p][s]
        at_bit = bit_of(axis, bit)
        half = sizes[p] // 2
        keep = lows[p] + at_bit * half
        give = lows[p] + (1 - at_bit) * half
        ref, cols = sums(p)
        i = p * deep + s
        sends[i][...] = ref[pl.ds(give, half), :, cols].astype(BF16)
        copies[p, s] = remote(sends[i], recvs[i], w_send.at[i], w_recv.at[i], partner(axis, bit))
        copies[p, s].start()
        lows[p], sizes[p] = keep, half

    def absorb(p, s):
        copies[p, s].wait()
        i = p * deep + s
        ref, cols = sums(p)
        at = pl.ds(lows[p], sizes[p])
        total = ref[at, :, cols] + recvs[i][...].astype(F32)
        if s + 1 < deep:
            ref[at, :, cols] = total
        elif p < parts:
            up_out[:, cols] = total[0, 0:own]
            down_out[:, cols] = total[0, own:]
        else:
            ag_hot[r] = total[0]

    for c in base_copies:
        c.wait()
    x_copy.wait()
    factors = jnp.concatenate([x_own[...], x_in[...]], axis=1)
    for c in range(CHUNKS):
        at = slice(c * wide, (c + 1) * wide)
        both = jnp.dot(factors, base[:, at], preferred_element_type=F32)
        up = both[0:rank // 2] * outw_ref[at].reshape(1, -1)
        down = both[rank // 2:]
        for i in range(parts // CHUNKS):
            p = c * (parts // CHUNKS) + i
            part, cols = slice(i * step, (i + 1) * step), slice(p * step, (p + 1) * step)
            for d in range(chips):
                rows_d = slice(d * own, (d + 1) * own)
                acc[plan[p][d], 0:own, cols] = up[rows_d, part]
                acc[plan[p][d], own:two, cols] = down[rows_d, part]
            launch(p, 0)

    for c in range(CHUNKS):
        at = slice(c * wide, (c + 1) * wide)
        gate = jnp.dot(low_b, up_ref[:, at], preferred_element_type=F32)
        gate = gate + (bias_ref[at].reshape(1, -1) + 1.0)
        grad = (lgrad * outw_ref[at].reshape(1, -1)) * gate + jnp.dot(
            g_low, down_ref[:, at], preferred_element_type=F32
        )
        for i in range(wide // LANES):
            f = (c * wide) // LANES + i - 1
            if f >= 0:
                grad_t[:, f * batch:(f + 1) * batch] = (
                    grad[:, i * LANES:(i + 1) * LANES].T.astype(BF16)
                )
    total = jnp.dot(
        grad_t[...], pick[...].reshape(feats * batch, cache), preferred_element_type=F32
    ).T
    tg_cold[...] = total[:cold].astype(BF16).reshape(tg_cold.shape)
    out_copies = []
    for k in range(1, n_table):
        to = table_peer(k)
        out_copies.append(
            remote(tg_cold.at[to[0]], ag_cold.at[r, t], c_send.at[k], c_recv.at[k], to)
        )
    for c in out_copies:
        c.start()
    ag_cold[r, t] = tg_cold[t]
    halves = total[cold:].reshape(slots, n_table, 2, two, EMB)
    other = jnp.where(is_first, halves[:, :, 1], halves[:, :, 0])
    mine = jnp.where(is_first, halves[:, :, 0], halves[:, :, 1])
    for o in range(n_table):
        for s in range(slots):
            hot_send[plan[parts][o * slots + s]] = other[s, o].astype(BF16)
            acc_hot[plan[parts][o * slots + s]] = mine[s, o]
    hot_pair = remote(hot_send, hot_recv, m_send.at[2], m_recv.at[2], mate)
    hot_pair.start()

    across = (t, lax.rem(r + n_rep // 2, n_rep))
    shares = []

    def hot_first():
        hot_pair.wait()
        acc_hot[...] = acc_hot[...] + hot_recv[...].astype(F32)
        launch(parts, 0)

    def share():
        for c in out_copies:
            c.wait()
        for n, to in enumerate((across, mate)):
            shares.append(remote(ag_cold.at[r], ag_cold.at[r], a_send.at[n], a_recv.at[n], to))
            shares[n].start()

    def forward():
        shares[0].wait()
        there = lax.rem(r + n_rep // 2, n_rep)
        shares.append(
            remote(ag_cold.at[there], ag_cold.at[there], a_send.at[2], a_recv.at[2], mate)
        )
        shares[2].start()

    mine_blocks = table_out.shape[0]
    first_block = r * mine_blocks

    def finish_cold():
        for c in id_shares:
            c.wait()
        shares[1].wait()
        shares[2].wait()
        total = [jnp.zeros((BLOCK, EMB), F32) for _ in range(mine_blocks)]
        for q in range(n_rep):
            for o in range(n_table):
                for w in range(wants):
                    ids = ag_ids[q, o, w:w + 1, :] - first_block
                    val = ag_cold[q, o, w].astype(F32)
                    for b in range(mine_blocks):
                        total[b] = total[b] + jnp.where(ids == b, val, 0.0)
        for b in range(mine_blocks):
            table_out[b] = total[b]

    hot_shares = []

    def share_hot():
        for k in range(1, n_rep):
            hot_shares.append(
                remote(ag_hot.at[r], ag_hot.at[r], g_send.at[k], g_recv.at[k], rep_peer(k))
            )
            hot_shares[k - 1].start()

    def finish_hot():
        for c in hot_shares:
            c.wait()
        val = ag_hot[...].reshape(slots, BLOCK, EMB)
        for b in range(mine_blocks):
            total = table_out[b]
            for h in range(slots):
                ids = jnp.where(hot_rows[h] >= 0, hot_rows[h] - first_block, -1)
                total = total + jnp.where(ids == b, val[h], 0.0)
            table_out[b] = total

    for s in range(deep):
        order = list(range(parts))
        order.insert(parts - s * parts // (deep - 1), parts)
        for n, p in enumerate(order):
            absorb(p, s)
            if s + 1 < deep:
                launch(p, s + 1)
            elif p == parts:
                share_hot()
            if s == 0 and n == 2:
                hot_first()
            if s == 0 and n == 6:
                share()
            if s == 1 and n == 4:
                forward()
            if s == 2 and n == 6:
                finish_cold()
    finish_hot()


def whole(
    plan, stages, n_table, n_rep, want, hot_ids, count, emb, ids, weight, length, dense, labels,
    up, down, bias, outw, bw, bb,
):
    feats, bag, batch = ids.shape
    padded = -(-feats * bag // LANES) * LANES
    devices = n_table * n_rep
    rank, width = up.shape
    own = rank // devices
    two, chips = 2 * own, devices // 2
    wants, slots = want.shape[2], hot_ids.shape[1]
    cache = n_table * (wants + slots) * BLOCK
    step = width // PARTS
    mine = emb.shape[0] // BLOCK // n_rep
    shapes = []
    for p, part in enumerate(stages):
        size = chips
        for _ in part:
            size //= 2
            shapes.append(pltpu.VMEM((size, two, step if p < PARTS else EMB), BF16))
    dma = pltpu.SemaphoreType.DMA
    one, many = pl.BlockSpec(memory_space=pltpu.SMEM), pl.BlockSpec(memory_space=pltpu.HBM)
    return pl.pallas_call(
        functools.partial(whole_kernel, plan, stages, n_table, n_rep, len(shapes)),
        out_shape=[
            pltpu.VMEM((own, width), F32),
            pltpu.VMEM((own, width), F32),
            pltpu.VMEM((mine, BLOCK, EMB), F32),
        ],
        in_specs=[one] * 3 + [many] * 12,
        out_specs=vmem(3),
        scratch_shapes=[
            pltpu.VMEM(a.shape, a.dtype)
            for a in (emb, ids, weight, length, dense, labels, up, down, bias, outw, bw, bb)
        ] + [
            pltpu.VMEM((n_table, wants, LANES), jnp.int32),
            pltpu.VMEM((n_table, wants, LANES), jnp.int32),
            pltpu.VMEM((n_table, wants, BLOCK, EMB), BF16),
            pltpu.VMEM((slots, BLOCK, EMB), BF16),
            pltpu.VMEM((n_table, wants, BLOCK, EMB), BF16),
            pltpu.VMEM((slots, n_table, BLOCK, EMB), BF16),
            pltpu.VMEM((feats, batch, cache), BF16),
            pltpu.VMEM((feats, batch, cache), BF16),
            pltpu.VMEM((2 * batch, width), BF16),
            pltpu.VMEM((batch, width), F32),
            pltpu.VMEM((batch, width), BF16),
            pltpu.VMEM((EMB, feats * batch), BF16),
            pltpu.VMEM((batch, padded), F32),
            pltpu.VMEM((batch, padded), F32),
            pltpu.VMEM((padded, batch), F32),
            pltpu.VMEM((rank, batch), BF16),
            pltpu.VMEM((rank, batch), BF16),
            pltpu.VMEM((rank, batch), BF16),
            pltpu.VMEM((chips, two, width), F32),
            pltpu.VMEM((chips, two, EMB), F32),
            pltpu.VMEM((chips, two, EMB), BF16),
            pltpu.VMEM((chips, two, EMB), BF16),
            pltpu.VMEM((n_table, wants, BLOCK, EMB), BF16),
            pltpu.VMEM((n_rep, n_table, wants, BLOCK, EMB), BF16),
            pltpu.VMEM((n_rep, two, EMB), F32),
            pltpu.VMEM((n_rep, n_table, wants, LANES), jnp.int32),
        ] + shapes + shapes + [dma((12,))] + [dma((n_table,))] * 6 + [dma((CHUNKS,))] * 2
        + [dma((len(shapes),))] * 2 + [dma((n_table,))] * 2 + [dma((3,))] * 2
        + [dma((n_rep,))] * 4 + [dma((3,))] * 2,
        compiler_params=pltpu.CompilerParams(
            collective_id=0, has_side_effects=True, vmem_limit_bytes=60 * 2**20
        ),
        name="whole",
    )(want, hot_ids, count, emb, ids, weight, length, dense, labels, up, down, bias, outw, bw, bb)


def finish_kernel(*refs):
    n = len(refs) // 2
    sem = refs[-1]
    copies = [
        pltpu.make_async_copy(refs[i], refs[n + i], sem.at[i]) for i in range(n)
    ]
    for c in copies:
        c.start()
    for c in copies:
        c.wait()


def finish(*arrays):
    many = [pl.BlockSpec(memory_space=pltpu.VMEM)] * len(arrays)
    outs = [pl.BlockSpec(memory_space=pltpu.HBM)] * len(arrays)
    return pl.pallas_call(
        finish_kernel,
        out_shape=[jax.ShapeDtypeStruct(a.shape, a.dtype) for a in arrays],
        in_specs=many,
        out_specs=outs,
        scratch_shapes=[pltpu.SemaphoreType.DMA((len(arrays),))],
        name="finish",
    )(*arrays)


def make_stages(n_table, n_rep, parts):
    rep = [("replica", b) for b in range(1, n_rep.bit_length() - 1)]
    tab = [("table", b) for b in range(n_table.bit_length() - 1)]
    bits = rep + tab
    tail = bits[:-1]
    turned = [tail[p % len(tail):] + tail[:p % len(tail)] for p in range(parts + 1)]
    return [part + bits[-1:] for part in turned]


def places(stages, n_rep, chips):
    plan = []
    pairs = n_rep // 2
    for part in stages:
        row = []
        for d in range(chips):
            at = 0
            for axis, bit in part:
                number = d // pairs if axis == "table" else (d % pairs) * 2
                at = at * 2 + (number >> bit) % 2
            row.append(at)
        plan.append(row)
    return plan


def fast_local(
    emb_table, cross_up, cross_down, cross_bias, out_weight, bottom_weight, bottom_bias,
    dense_in, labels, lookup_ids, bag_weight, bag_length, want_blocks, hot_blocks, hot_count,
):
    owners, reps = lax.axis_size("table"), lax.axis_size("replica")
    stages = make_stages(owners, reps, PARTS)
    plan = places(stages, reps, owners * reps // 2)
    up, down, table = whole(
        plan, stages, owners, reps, want_blocks.transpose(0, 1, 3, 2), hot_blocks, hot_count, emb_table,
        lookup_ids.transpose(1, 2, 0), bag_weight.transpose(1, 2, 0), bag_length.T,
        dense_in.T, labels[None], cross_up, cross_down, cross_bias, out_weight,
        bottom_weight, bottom_bias[None],
    )
    up, down, table = [pltpu.with_memory_space_constraint(a, pltpu.VMEM) for a in (up, down, table)]
    u, d, t = finish(up, down, table)
    return u, d, t.reshape(-1, EMB)


def local_step(
    cached_rows,
    dense_dev,
    labels_dev,
    ids_dev,
    weight_dev,
    length_dev,
    cross_up,
    cross_down,
    cross_bias,
    out_weight,
    bottom_weight,
    bottom_bias,
):
    batch = ids_dev.shape[0]
    width = cached_rows.shape[1]
    gathered = cached_rows[ids_dev].astype(jnp.float32)
    slots = jnp.arange(ids_dev.shape[2], dtype=jnp.int32)
    bag_coef = jnp.where(
        slots[None, None, :] < length_dev[:, :, None], weight_dev, jnp.zeros((), jnp.float32)
    )
    pooled = jnp.sum(bag_coef[..., None] * gathered, axis=2)
    bottom = jax.nn.relu(
        jnp.dot(dense_dev, bottom_weight, precision=lax.Precision.HIGHEST) + bottom_bias
    )
    cross_base = jnp.concatenate([bottom, pooled.reshape(batch, -1)], 1).astype(jnp.bfloat16)
    low_rank = lax.dot_general(
        cross_base, cross_down, (((1,), (1,)), ((), ())), preferred_element_type=jnp.float32
    ).astype(jnp.bfloat16)
    cross_gate = jnp.dot(low_rank, cross_up, preferred_element_type=jnp.float32) + cross_bias
    base_wide = cross_base.astype(jnp.float32)
    crossed = base_wide * cross_gate + base_wide
    logits = jnp.dot(crossed, out_weight, precision=lax.Precision.HIGHEST)
    logit_grad = jax.nn.sigmoid(logits) - labels_dev.astype(jnp.float32)
    grad_crossed = logit_grad[:, None] * out_weight[None, :]
    g_cross = (grad_crossed * base_wide).astype(jnp.bfloat16)
    g_low = lax.dot_general(
        g_cross, cross_up, (((1,), (1,)), ((), ())), preferred_element_type=jnp.float32
    ).astype(jnp.bfloat16)
    up_part = lax.dot_general(
        low_rank, g_cross, (((0,), (0,)), ((), ())), preferred_element_type=jnp.float32
    )
    down_part = lax.dot_general(
        g_low, cross_base, (((0,), (0,)), ((), ())), preferred_element_type=jnp.float32
    )
    grad_base = grad_crossed * (cross_gate + 1.0) + jnp.dot(
        g_low, cross_down, preferred_element_type=jnp.float32
    )
    grad_pooled = grad_base[:, width:].reshape(batch, -1, width)
    contrib = bag_coef[..., None] * grad_pooled[:, :, None, :]
    cache_grad = (
        jnp.zeros(cached_rows.shape, jnp.float32)
        .at[ids_dev.reshape(-1)]
        .add(contrib.reshape(-1, width))
    )
    return (up_part, down_part, cache_grad)


def plain_local(
    emb_table,
    cross_up,
    cross_down,
    cross_bias,
    out_weight,
    bottom_weight,
    bottom_bias,
    dense_in,
    labels,
    lookup_ids,
    bag_weight,
    bag_length,
    want_blocks,
    hot_blocks,
    hot_count,
):
    owners = lax.axis_size("table")
    blocks = emb_table.reshape(-1, BLOCK, EMB)
    block_total = blocks.shape[0]
    wanted = want_blocks.reshape(owners, want_blocks.shape[3])
    asked_for = lax.all_to_all(wanted, "table", split_axis=0, concat_axis=0, tiled=True)
    flat = emb_table.reshape(block_total, -1)
    numbers = jnp.arange(block_total, dtype=jnp.int32)

    def take(ids):
        pick = (ids.reshape(-1)[:, None] == numbers[None, :]).astype(jnp.bfloat16)
        rows = jnp.dot(pick, flat, preferred_element_type=jnp.float32).astype(jnp.bfloat16)
        return rows.reshape(ids.shape + (BLOCK, EMB))

    served = take(asked_for)
    cold_rows = lax.all_to_all(served, "table", split_axis=0, concat_axis=0, tiled=True)
    slot_count = hot_blocks.shape[1]
    alive = jnp.arange(slot_count, dtype=jnp.int32) < hot_count[0]
    own_hot = jnp.where(alive[:, None, None], take(hot_blocks[0]), jnp.zeros((), jnp.bfloat16))
    hot_rows = lax.all_gather(own_hot[:, None], "table", axis=1, tiled=True)
    cold_count = cold_rows.shape[0] * cold_rows.shape[1] * BLOCK
    cached_rows = jnp.concatenate([cold_rows.reshape(-1, EMB), hot_rows.reshape(-1, EMB)], 0)
    up_part, down_part, cache_grad = local_step(
        cached_rows,
        dense_in,
        labels,
        lookup_ids,
        bag_weight,
        bag_length,
        cross_up,
        cross_down,
        cross_bias,
        out_weight,
        bottom_weight,
        bottom_bias,
    )
    cold_grad = cache_grad[:cold_count].reshape(cold_rows.shape).astype(jnp.bfloat16)
    returned = lax.all_to_all(cold_grad, "table", split_axis=0, concat_axis=0, tiled=True)
    hot_grad = cache_grad[cold_count:].reshape(hot_rows.shape)
    hot_sums = lax.psum_scatter(hot_grad, "table", scatter_dimension=1, tiled=True)[:, 0]
    block_ids = jnp.arange(block_total, dtype=jnp.int32)
    cold_pick = (asked_for.reshape(-1)[:, None] == block_ids[None, :]).astype(jnp.bfloat16)
    hot_pick = ((hot_blocks[0][:, None] == block_ids[None, :]) & alive[:, None]).astype(jnp.float32)
    block_grad = lax.dot_general(
        cold_pick,
        returned.reshape(cold_pick.shape[0], -1),
        (((0,), (0,)), ((), ())),
        preferred_element_type=jnp.float32,
    )
    block_grad = block_grad + lax.dot_general(
        hot_pick,
        hot_sums.reshape(slot_count, -1),
        (((0,), (0,)), ((), ())),
        precision=lax.Precision.HIGHEST,
    )
    table_grad = lax.psum_scatter(
        block_grad.reshape(-1, EMB), "replica", scatter_dimension=0, tiled=True
    )
    up_grad, down_grad = (
        lax.psum_scatter(up_part, ("table", "replica"), scatter_dimension=0, tiled=True),
        lax.psum_scatter(down_part, ("table", "replica"), scatter_dimension=0, tiled=True),
    )
    return (up_grad, down_grad, table_grad)


def choose(mesh, *args):
    devices = mesh.shape["table"] * mesh.shape["replica"]
    powers = all(n > 1 and n & (n - 1) == 0 for n in mesh.shape.values())
    rank, width = args[1].shape
    ids, want, hot = args[9], args[12], args[13]
    cache = mesh.shape["table"] * (want.shape[3] + hot.shape[1]) * BLOCK
    picked = 2 * ids.shape[0] * ids.shape[1] * cache
    whole_tiles = rank % (devices * SUBLANES) == 0 and width % (PARTS * LANES) == 0
    reps = mesh.shape["replica"]
    even = 2 * rank // devices * reps == hot.shape[1] * BLOCK and reps == 2 * hot.shape[1]
    if powers and whole_tiles and even and ids.shape[0] == LANES and picked < 2**23:
        return fast_local(*args)
    return plain_local(*args)


def solution(mesh):
    local = functools.partial(choose, mesh)
    placed = (
        P("table", None),
        P(),
        P(),
        P(),
        P(),
        P(),
        P(),
        P(("table", "replica"), None),
        P(("table", "replica")),
        P(("table", "replica"), None, None),
        P(("table", "replica"), None, None),
        P(("table", "replica"), None),
        P("table", "replica", None, None),
        P("table", None),
        P("table"),
    )
    return jax.shard_map(
        local,
        mesh=mesh,
        in_specs=placed,
        out_specs=(
            P(("table", "replica"), None),
            P(("table", "replica"), None),
            P(("table", "replica"), None),
        ),
        check_vma=False,
    )
```

```python
import functools

import jax
import jax.numpy as jnp
from jax import lax
from jax.experimental import pallas as pl
from jax.experimental.pallas import tpu as pltpu
from jax.sharding import PartitionSpec as P

EMB = 128
BLOCK = 32
LANES = 128
SUBLANES = 8
MESH = pl.DeviceIdType.MESH
CHUNKS = 3
PARTS = 9
EARLY = 0
SHARE, FORWARD, FINISH = (1, 8), (2, 8), (3, 6)
HOT_AFTER = (5, 2, 0, 0)
F32 = jnp.float32
BF16 = jnp.bfloat16


def vmem(n):
    return [pl.BlockSpec(memory_space=pltpu.VMEM)] * n


def pick_rows(ids, emb_ref):
    total = emb_ref.shape[0]
    tiles = total // LANES
    row = lax.broadcasted_iota(jnp.int32, (BLOCK, LANES), 0)
    lane = lax.broadcasted_iota(jnp.int32, (BLOCK, LANES), 1)
    parts = []
    for block in ids:
        want = block * BLOCK + row
        parts.append(
            jnp.concatenate(
                [jnp.where(want == lane + LANES * c, 1.0, 0.0) for c in range(tiles)], axis=1
            )
        )
    pick = jnp.concatenate(parts, axis=0).astype(BF16)
    return jnp.dot(pick, emb_ref[...], preferred_element_type=F32).astype(BF16)


def whole_kernel(
    plan, stages, n_table, n_rep, buffers,
    want_ref, hot_ids_ref, count_ref, emb_hbm, ids_hbm, weight_hbm, length_hbm, dense_hbm,
    label_hbm, up_hbm, down_hbm, bias_hbm, outw_hbm, bw_hbm, bb_hbm,
    up_out, down_out, table_out,
    emb_ref, ids_ref, weight_ref, length_ref, dense_ref, label_ref, up_ref, down_ref,
    bias_ref, outw_ref, bw_ref, bb_ref, want_v, ask, serve, own_hot, cold_in, hot_in,
    pick, pick_low, base, part_sum, bow, grad_t, ids_cols, coef_cols, turn,
    down_t, up_t, x_own, x_send, x_in, acc, acc_hot, hot_send, hot_recv, fold_send, fold_recv, hot_all,
    hot_there, tg_cold, ag_cold, ag_ids,
    *rest,
):
    sends = rest[:buffers]
    recvs = rest[buffers:2 * buffers]
    (load_sem, id_send, id_recv, hs_send, hs_recv, cs_send, cs_recv, b_send, b_recv,
     w_send, w_recv, c_send, c_recv, a_send, a_recv, i_send, i_recv, f_send, f_recv,
     g_send, g_recv, m_send, m_recv) = rest[2 * buffers:]
    t = lax.axis_index("table")
    r = lax.axis_index("replica")
    wants = serve.shape[1]
    slots = own_hot.shape[0]
    feats, batch, cache = pick.shape
    bag = ids_ref.shape[1]
    width = base.shape[1]
    group = 16
    core = lax.rem(r, 2)
    mate = (t, r + 1 - 2 * core)

    def table_peer(k):
        return (lax.rem(t + k, n_table), r)

    def rep_peer(k):
        return (t, lax.rem(r + k, n_rep))

    def remote(src, dst, send, recv, device):
        return pltpu.make_async_remote_copy(
            src_ref=src, dst_ref=dst, send_sem=send, recv_sem=recv,
            device_id=device, device_id_type=MESH,
        )

    barrier = pltpu.get_barrier_semaphore()
    for k in range(1, n_table):
        pl.semaphore_signal(barrier, inc=1, device_id=table_peer(k), device_id_type=MESH)
    for k in range(1, n_rep):
        pl.semaphore_signal(barrier, inc=1, device_id=rep_peer(k), device_id_type=MESH)
    loads = [
        pltpu.make_async_copy(src, dst, load_sem.at[i])
        for i, (src, dst) in enumerate((
            (emb_hbm, emb_ref), (ids_hbm, ids_ref), (weight_hbm, weight_ref),
            (length_hbm, length_ref), (dense_hbm, dense_ref), (label_hbm, label_ref),
            (bw_hbm, bw_ref), (bb_hbm, bb_ref), (bias_hbm, bias_ref), (outw_hbm, outw_ref),
            (down_hbm, down_ref), (up_hbm, up_ref),
        ))
    ]
    for c in loads:
        c.start()
    for p in range(n_table):
        for w in range(wants):
            want_v[p, w:w + 1] = jnp.full((1, LANES), want_ref[0, 0, w, p], jnp.int32)
    ask[t] = want_v[t]
    hot_rows = []
    for s in range(slots):
        block = jnp.where(s < count_ref[0], hot_ids_ref[0, s], -1)
        hot_rows.append(jnp.full((1, LANES), block, jnp.int32))

    loads[0].wait()
    own_hot[...] = pick_rows(hot_rows, emb_ref).reshape(slots, BLOCK, EMB)
    half_block = pl.ds(pl.multiple_of(core * (BLOCK // 2), BLOCK // 2), BLOCK // 2)
    hot_in[:, t, half_block] = own_hot[:, half_block]
    for c in loads[1:10]:
        c.wait()
    turn[...] = jnp.zeros_like(turn)
    for f in range(feats):
        turn[f * bag:(f + 1) * bag, :] = ids_ref[f].astype(F32)
    ids_cols[...] = turn[...].T
    spot = lax.broadcasted_iota(jnp.int32, (bag, batch), 0)
    for f in range(feats):
        live = spot < length_ref[f:f + 1, :]
        turn[f * bag:(f + 1) * bag, :] = jnp.where(live, weight_ref[f], 0.0)
    coef_cols[...] = turn[...].T

    def build(first, last):
        @pl.loop(first, last)
        def _(g):
            at = pl.ds(pl.multiple_of(g * group, group), group)
            ids = ids_cols[at, :]
            coef = coef_cols[at, :]
            lane = lax.broadcasted_iota(jnp.int32, (group, cache), 1).astype(F32)
            for f in range(feats):
                total = None
                for l in range(bag):
                    j = f * bag + l
                    term = jnp.where(ids[:, j:j + 1] == lane, coef[:, j:j + 1], 0.0)
                    total = term if total is None else total + term
                high = total.astype(BF16)
                pick[f, at, :] = high
                pick_low[f, at, :] = (total - high.astype(F32)).astype(BF16)

    build(0, EARLY)
    pl.semaphore_wait(barrier, n_table - 1 + n_rep - 1)

    id_copies = [
        remote(want_v.at[table_peer(k)[0]], ask.at[t], id_send.at[k], id_recv.at[k], table_peer(k))
        for k in range(1, n_table)
    ]
    hot_copies = [
        remote(own_hot.at[:, half_block], hot_in.at[:, t, half_block], hs_send.at[k],
               hs_recv.at[k], table_peer(k))
        for k in range(1, n_table)
    ]
    for c in id_copies + hot_copies:
        c.start()

    groups = batch // group
    first = groups * 5 // 8
    build(EARLY, first)
    for c in id_copies:
        c.wait()
    asked = [ask[p, w:w + 1, :] for p in range(n_table) for w in range(wants)]
    serve[...] = pick_rows(asked, emb_ref).reshape(n_table, wants, BLOCK, EMB)
    cold_copies = [
        remote(serve.at[table_peer(k)[0]], cold_in.at[t], cs_send.at[k], cs_recv.at[k],
               table_peer(k))
        for k in range(1, n_table)
    ]
    for c in cold_copies:
        c.start()
    for c in hot_copies:
        c.wait()
    hot_mate = remote(
        hot_in.at[:, :, half_block], hot_in.at[:, :, half_block], m_send.at[0], m_recv.at[0], mate
    )
    hot_mate.start()
    cold_in[t] = serve[t]
    ag_ids[r] = ask[...]
    id_shares = [
        remote(ask, ag_ids.at[r], i_send.at[k], i_recv.at[k], rep_peer(k)) for k in range(1, n_rep)
    ]
    for c in id_shares:
        c.start()
    build(first, groups)

    bottom = jnp.zeros((batch, EMB), F32) + bb_ref[...]
    features = dense_ref.shape[0]
    turn[0:features, :] = dense_ref[...]
    turn[features:features + 1, :] = label_ref[...].astype(F32)
    dense = turn[...].T
    label = dense[:, features:features + 1]
    for j in range(features):
        bottom = bottom + dense[:, j:j + 1] * bw_ref[j:j + 1, :]
    lsum = jnp.zeros((batch, LANES), F32)

    def settle(lsum, j, value):
        cols = slice(j * EMB, (j + 1) * EMB)
        b = value.astype(BF16)
        base[0:batch, cols] = b
        x = b.astype(F32) * outw_ref[cols].reshape(1, -1)
        bow[:, cols] = x.astype(BF16)
        return lsum + x * (bias_ref[cols].reshape(1, -1) + 1.0)

    lsum = settle(lsum, 0, jnp.maximum(bottom, 0.0))
    cold = n_table * wants * BLOCK
    some = 2 if feats % 2 == 0 else 1

    def pool(f, cols, rows):
        at = slice(f, f + some)
        return jnp.dot(
            pick[at, :, cols].reshape(some * batch, -1), rows, preferred_element_type=F32
        ) + jnp.dot(
            pick_low[at, :, cols].reshape(some * batch, -1), rows, preferred_element_type=F32
        )

    for c in loads[10:]:
        c.wait()
    def turn_weights(j):
        cols = slice(j * EMB, (j + 1) * EMB)
        down_t[cols] = down_ref[:, cols].T
        up_t[cols] = up_ref[:, cols].T

    hot_mate.wait()
    rows = hot_in[...].reshape(cache - cold, EMB)
    for f in range(0, feats, some):
        pooled = pool(f, slice(cold, cache), rows)
        for i in range(some):
            part_sum[:, (f + i) * EMB:(f + i + 1) * EMB] = pooled[i * batch:(i + 1) * batch]
            turn_weights(f + i)
    turn_weights(feats)
    for c in cold_copies:
        c.wait()
    rows = cold_in[...].reshape(cold, EMB)
    wide = width // CHUNKS
    base_copies = []
    for f in range(0, feats, some):
        pooled = pool(f, slice(0, cold), rows)
        for i in range(some):
            before = part_sum[:, (f + i) * EMB:(f + i + 1) * EMB]
            lsum = settle(lsum, f + i + 1, pooled[i * batch:(i + 1) * batch] + before)
        n = len(base_copies)
        while n < CHUNKS and (f + some + 1) * EMB >= (n + 1) * wide:
            cols = slice(n * wide, (n + 1) * wide)
            base_copies.append(remote(
                base.at[0:batch, cols], base.at[batch:2 * batch, cols], b_send.at[n],
                b_recv.at[n], mate,
            ))
            base_copies[n].start()
            n += 1

    low = jnp.dot(base[0:batch], down_t[...], preferred_element_type=F32)
    high = jnp.dot(bow[...], up_t[...], preferred_element_type=F32)
    low_b = low.astype(BF16)
    prod = low_b.astype(F32) * high
    rank = prod.shape[1]
    for i in range(rank // LANES):
        lsum = lsum + prod[:, i * LANES:(i + 1) * LANES]
    logit = jnp.sum(lsum, axis=1, keepdims=True)
    lgrad = jax.nn.sigmoid(logit) - label
    g_low_f = high * lgrad
    g_low = g_low_f.astype(BF16)
    chips, two = acc.shape[0], acc.shape[1]
    own = two // 2
    turned = jnp.concatenate([low * lgrad, g_low_f], axis=1).T
    turned = turned.reshape(2, chips, 2, own, batch)
    is_first = core == 0
    mine = jnp.where(is_first, turned[:, :, 0], turned[:, :, 1])
    other = jnp.where(is_first, turned[:, :, 1], turned[:, :, 0])
    x_send[...] = other.reshape(rank, batch).astype(BF16)
    x_copy = remote(x_send, x_in, m_send.at[1], m_recv.at[1], mate)
    x_copy.start()
    x_own[...] = mine.reshape(rank, batch).astype(BF16)

    def bit_of(axis, bit):
        return lax.rem((t if axis == "table" else r) // (1 << bit), 2)

    def partner(axis, bit):
        shift = (1 - 2 * bit_of(axis, bit)) * (1 << bit)
        return (t + shift, r) if axis == "table" else (t, r + shift)

    parts = len(plan)
    step = width // parts
    lows = [0] * parts
    sizes = [chips] * parts
    copies = {}
    deep = len(stages[0])

    def launch(p, s):
        axis, bit = stages[p][s]
        at_bit = bit_of(axis, bit)
        half = sizes[p] // 2
        keep = lows[p] + at_bit * half
        give = lows[p] + (1 - at_bit) * half
        cols = slice(p * step, (p + 1) * step)
        i = p * deep + s
        sends[i][...] = acc[pl.ds(give, half), :, cols].astype(BF16)
        copies[p, s] = remote(sends[i], recvs[i], w_send.at[i], w_recv.at[i], partner(axis, bit))
        copies[p, s].start()
        lows[p], sizes[p] = keep, half

    def absorb(p, s):
        copies[p, s].wait()
        i = p * deep + s
        cols = slice(p * step, (p + 1) * step)
        at = pl.ds(lows[p], sizes[p])
        total = acc[at, :, cols] + recvs[i][...].astype(F32)
        if s + 1 < deep:
            acc[at, :, cols] = total
        else:
            up_out[:, cols] = total[0, 0:own]
            down_out[:, cols] = total[0, own:]

    for c in base_copies:
        c.wait()
    x_copy.wait()
    factors = jnp.concatenate([x_own[...], x_in[...]], axis=1)
    for c in range(CHUNKS):
        at = slice(c * wide, (c + 1) * wide)
        both = jnp.dot(factors, base[:, at], preferred_element_type=F32)
        up = both[0:rank // 2] * outw_ref[at].reshape(1, -1)
        down = both[rank // 2:]
        for i in range(parts // CHUNKS):
            p = c * (parts // CHUNKS) + i
            part, cols = slice(i * step, (i + 1) * step), slice(p * step, (p + 1) * step)
            for d in range(chips):
                rows_d = slice(d * own, (d + 1) * own)
                acc[plan[p][d], 0:own, cols] = up[rows_d, part]
                acc[plan[p][d], own:two, cols] = down[rows_d, part]
            launch(p, 0)

    for c in range(CHUNKS):
        at = slice(c * wide, (c + 1) * wide)
        gate = jnp.dot(low_b, up_ref[:, at], preferred_element_type=F32)
        gate = gate + (bias_ref[at].reshape(1, -1) + 1.0)
        grad = (lgrad * outw_ref[at].reshape(1, -1)) * gate + jnp.dot(
            g_low, down_ref[:, at], preferred_element_type=F32
        )
        for i in range(wide // LANES):
            f = (c * wide) // LANES + i - 1
            if f >= 0:
                grad_t[:, f * batch:(f + 1) * batch] = (
                    grad[:, i * LANES:(i + 1) * LANES].T.astype(BF16)
                )
    total = jnp.dot(
        grad_t[...], pick[...].reshape(feats * batch, cache), preferred_element_type=F32
    ).T
    tg_cold[...] = total[:cold].astype(BF16).reshape(tg_cold.shape)
    out_copies = []
    for k in range(1, n_table):
        to = table_peer(k)
        out_copies.append(
            remote(tg_cold.at[to[0]], ag_cold.at[r, t], c_send.at[k], c_recv.at[k], to)
        )
    for c in out_copies:
        c.start()
    ag_cold[r, t] = tg_cold[t]
    halves = total[cold:].reshape(slots, n_table, 2, BLOCK // 2, EMB)
    other = jnp.where(is_first, halves[:, :, 1], halves[:, :, 0])
    mine = jnp.where(is_first, halves[:, :, 0], halves[:, :, 1])
    folds = n_table.bit_length() - 1
    for o in range(n_table):
        at = sum(((o >> b) & 1) << (folds - 1 - b) for b in range(folds))
        for s in range(slots):
            hot_send[at, s] = other[s, o].astype(BF16)
            acc_hot[at, s] = mine[s, o]
    hot_pair = remote(hot_send, hot_recv, m_send.at[2], m_recv.at[2], mate)
    hot_pair.start()
    hot_at = [0, n_table]
    hot_copies = []

    def hot_launch():
        b = len(hot_copies)
        half = hot_at[1] // 2
        at_bit = bit_of("table", b)
        keep, give = hot_at[0] + at_bit * half, hot_at[0] + (1 - at_bit) * half
        span = pl.ds(n_table - 2 * half, half)
        fold_send[span] = acc_hot[pl.ds(give, half)].astype(BF16)
        hot_copies.append(remote(
            fold_send.at[span], fold_recv.at[span], f_send.at[b], f_recv.at[b],
            partner("table", b),
        ))
        hot_copies[b].start()
        hot_at[:] = [keep, half]

    def hot_absorb():
        hot_copies[-1].wait()
        at, half = pl.ds(hot_at[0], hot_at[1]), hot_at[1]
        span = slice(n_table - 2 * half, n_table - half)
        acc_hot[at] = acc_hot[at] + fold_recv[span].astype(F32)

    rep_bits = n_rep.bit_length() - 1
    hot_shares = []

    def hot_step(n):
        if n < folds:
            hot_absorb()
            if n + 1 < folds:
                hot_launch()
            else:
                hot_all[0] = acc_hot[hot_at[0]]
        elif n < folds + rep_bits - 1:
            hot_shares[-1].wait()
            k = n - folds
            hot_all[k + 1] = hot_all[k] + hot_there[k]
        k = n - folds + 1
        if 0 <= k < rep_bits:
            to = partner("replica", k + 1) if k + 1 < rep_bits else mate
            hot_shares.append(
                remote(hot_all.at[k], hot_there.at[k], g_send.at[k], g_recv.at[k], to)
            )
            hot_shares[k].start()

    hot_pair.wait()
    acc_hot[...] = acc_hot[...] + hot_recv[...].astype(F32)
    hot_launch()

    across = (t, lax.rem(r + n_rep // 2, n_rep))
    shares = []

    def share():
        for c in out_copies:
            c.wait()
        for n, to in enumerate((across, mate)):
            shares.append(remote(ag_cold.at[r], ag_cold.at[r], a_send.at[n], a_recv.at[n], to))
            shares[n].start()

    def forward():
        shares[0].wait()
        there = lax.rem(r + n_rep // 2, n_rep)
        shares.append(
            remote(ag_cold.at[there], ag_cold.at[there], a_send.at[2], a_recv.at[2], mate)
        )
        shares[2].start()

    mine_blocks = table_out.shape[0]
    first_block = r * mine_blocks

    def finish_cold():
        for c in id_shares:
            c.wait()
        shares[1].wait()
        shares[2].wait()
        total = [jnp.zeros((BLOCK, EMB), F32) for _ in range(mine_blocks)]
        for q in range(n_rep):
            for o in range(n_table):
                for w in range(wants):
                    ids = ag_ids[q, o, w:w + 1, :] - first_block
                    val = ag_cold[q, o, w].astype(F32)
                    for b in range(mine_blocks):
                        total[b] = total[b] + jnp.where(ids == b, val, 0.0)
        for b in range(mine_blocks):
            table_out[b] = total[b]

    def finish_hot():
        hot_shares[-1].wait()
        ours, theirs = hot_all[rep_bits - 1], hot_there[rep_bits - 1]
        for b in range(mine_blocks):
            total = table_out[b]
            for h in range(slots):
                ids = jnp.where(hot_rows[h] >= 0, hot_rows[h] - first_block, -1)
                val = jnp.concatenate([
                    jnp.where(is_first, ours[h], theirs[h]), jnp.where(is_first, theirs[h], ours[h])
                ], axis=0)
                total = total + jnp.where(ids == b, val, 0.0)
            table_out[b] = total

    hot_steps = list(range(folds + rep_bits - 1))
    for s in range(deep):
        for p in range(parts):
            absorb(p, s)
            if s + 1 < deep:
                launch(p, s + 1)
            if hot_steps and p == HOT_AFTER[min(s, len(HOT_AFTER) - 1)]:
                hot_step(hot_steps.pop(0))
            if (s, p) == SHARE:
                share()
            if (s, p) == FORWARD:
                forward()
            if (s, p) == FINISH:
                finish_cold()
    while hot_steps:
        hot_step(hot_steps.pop(0))
    finish_hot()


def whole(
    plan, stages, n_table, n_rep, want, hot_ids, count, emb, ids, weight, length, dense, labels,
    up, down, bias, outw, bw, bb,
):
    feats, bag, batch = ids.shape
    padded = -(-feats * bag // LANES) * LANES
    devices = n_table * n_rep
    rank, width = up.shape
    own = rank // devices
    two, chips = 2 * own, devices // 2
    wants, slots = want.shape[2], hot_ids.shape[1]
    cache = n_table * (wants + slots) * BLOCK
    step = width // PARTS
    mine = emb.shape[0] // BLOCK // n_rep
    shapes = []
    for part in stages:
        size = chips
        for _ in part:
            size //= 2
            shapes.append(pltpu.VMEM((size, two, step), BF16))
    dma = pltpu.SemaphoreType.DMA
    one, many = pl.BlockSpec(memory_space=pltpu.SMEM), pl.BlockSpec(memory_space=pltpu.HBM)
    return pl.pallas_call(
        functools.partial(whole_kernel, plan, stages, n_table, n_rep, len(shapes)),
        out_shape=[
            pltpu.VMEM((own, width), F32),
            pltpu.VMEM((own, width), F32),
            pltpu.VMEM((mine, BLOCK, EMB), F32),
        ],
        in_specs=[one] * 3 + [many] * 12,
        out_specs=vmem(3),
        scratch_shapes=[
            pltpu.VMEM(a.shape, a.dtype)
            for a in (emb, ids, weight, length, dense, labels, up, down, bias, outw, bw, bb)
        ] + [
            pltpu.VMEM((n_table, wants, LANES), jnp.int32),
            pltpu.VMEM((n_table, wants, LANES), jnp.int32),
            pltpu.VMEM((n_table, wants, BLOCK, EMB), BF16),
            pltpu.VMEM((slots, BLOCK, EMB), BF16),
            pltpu.VMEM((n_table, wants, BLOCK, EMB), BF16),
            pltpu.VMEM((slots, n_table, BLOCK, EMB), BF16),
            pltpu.VMEM((feats, batch, cache), BF16),
            pltpu.VMEM((feats, batch, cache), BF16),
            pltpu.VMEM((2 * batch, width), BF16),
            pltpu.VMEM((batch, width), F32),
            pltpu.VMEM((batch, width), BF16),
            pltpu.VMEM((EMB, feats * batch), BF16),
            pltpu.VMEM((batch, padded), F32),
            pltpu.VMEM((batch, padded), F32),
            pltpu.VMEM((padded, batch), F32),
            pltpu.VMEM((width, rank), BF16),
            pltpu.VMEM((width, rank), BF16),
            pltpu.VMEM((rank, batch), BF16),
            pltpu.VMEM((rank, batch), BF16),
            pltpu.VMEM((rank, batch), BF16),
            pltpu.VMEM((chips, two, width), F32),
            pltpu.VMEM((n_table, slots, BLOCK // 2, EMB), F32),
        ] + [pltpu.VMEM((n_table, slots, BLOCK // 2, EMB), BF16)] * 4 + [
            pltpu.VMEM((n_rep.bit_length() - 1, slots, BLOCK // 2, EMB), F32),
            pltpu.VMEM((n_rep.bit_length() - 1, slots, BLOCK // 2, EMB), F32),
            pltpu.VMEM((n_table, wants, BLOCK, EMB), BF16),
            pltpu.VMEM((n_rep, n_table, wants, BLOCK, EMB), BF16),
            pltpu.VMEM((n_rep, n_table, wants, LANES), jnp.int32),
        ] + shapes + shapes + [dma((12,))] + [dma((n_table,))] * 6 + [dma((CHUNKS,))] * 2
        + [dma((len(shapes),))] * 2 + [dma((n_table,))] * 2 + [dma((3,))] * 2
        + [dma((n_rep,))] * 2 + [dma((n_table,))] * 2 + [dma((n_rep,))] * 2 + [dma((3,))] * 2,
        compiler_params=pltpu.CompilerParams(
            collective_id=0, has_side_effects=True, vmem_limit_bytes=60 * 2**20
        ),
        name="whole",
    )(want, hot_ids, count, emb, ids, weight, length, dense, labels, up, down, bias, outw, bw, bb)


def finish_kernel(*refs):
    n = len(refs) // 2
    sem = refs[-1]
    copies = [
        pltpu.make_async_copy(refs[i], refs[n + i], sem.at[i]) for i in range(n)
    ]
    for c in copies:
        c.start()
    for c in copies:
        c.wait()


def finish(*arrays):
    many = [pl.BlockSpec(memory_space=pltpu.VMEM)] * len(arrays)
    outs = [pl.BlockSpec(memory_space=pltpu.HBM)] * len(arrays)
    return pl.pallas_call(
        finish_kernel,
        out_shape=[jax.ShapeDtypeStruct(a.shape, a.dtype) for a in arrays],
        in_specs=many,
        out_specs=outs,
        scratch_shapes=[pltpu.SemaphoreType.DMA((len(arrays),))],
        name="finish",
    )(*arrays)


def make_stages(n_table, n_rep, parts):
    rep = [("replica", b) for b in range(1, n_rep.bit_length() - 1)]
    tab = [("table", b) for b in range(n_table.bit_length() - 1)]
    bits = rep + tab
    tail = bits[:-1]
    turned = [tail[p % len(tail):] + tail[:p % len(tail)] for p in range(parts)]
    swapped = [False for p in range(parts)]
    return [
        part[:-1] + bits[-1:] + part[-1:] if swap else part + bits[-1:]
        for part, swap in zip(turned, swapped)
    ]


def places(stages, n_rep, chips):
    plan = []
    pairs = n_rep // 2
    for part in stages:
        row = []
        for d in range(chips):
            at = 0
            for axis, bit in part:
                number = d // pairs if axis == "table" else (d % pairs) * 2
                at = at * 2 + (number >> bit) % 2
            row.append(at)
        plan.append(row)
    return plan


def fast_local(
    emb_table, cross_up, cross_down, cross_bias, out_weight, bottom_weight, bottom_bias,
    dense_in, labels, lookup_ids, bag_weight, bag_length, want_blocks, hot_blocks, hot_count,
):
    owners, reps = lax.axis_size("table"), lax.axis_size("replica")
    stages = make_stages(owners, reps, PARTS)
    plan = places(stages, reps, owners * reps // 2)
    up, down, table = whole(
        plan, stages, owners, reps, want_blocks.transpose(0, 1, 3, 2), hot_blocks, hot_count, emb_table,
        lookup_ids.transpose(1, 2, 0), bag_weight.transpose(1, 2, 0), bag_length.T,
        dense_in.T, labels[None], cross_up, cross_down, cross_bias, out_weight,
        bottom_weight, bottom_bias[None],
    )
    up, down, table = [pltpu.with_memory_space_constraint(a, pltpu.VMEM) for a in (up, down, table)]
    u, d, t = finish(up, down, table)
    return u, d, t.reshape(-1, EMB)


def local_step(
    cached_rows,
    dense_dev,
    labels_dev,
    ids_dev,
    weight_dev,
    length_dev,
    cross_up,
    cross_down,
    cross_bias,
    out_weight,
    bottom_weight,
    bottom_bias,
):
    batch = ids_dev.shape[0]
    width = cached_rows.shape[1]
    gathered = cached_rows[ids_dev].astype(jnp.float32)
    slots = jnp.arange(ids_dev.shape[2], dtype=jnp.int32)
    bag_coef = jnp.where(
        slots[None, None, :] < length_dev[:, :, None], weight_dev, jnp.zeros((), jnp.float32)
    )
    pooled = jnp.sum(bag_coef[..., None] * gathered, axis=2)
    bottom = jax.nn.relu(
        jnp.dot(dense_dev, bottom_weight, precision=lax.Precision.HIGHEST) + bottom_bias
    )
    cross_base = jnp.concatenate([bottom, pooled.reshape(batch, -1)], 1).astype(jnp.bfloat16)
    low_rank = lax.dot_general(
        cross_base, cross_down, (((1,), (1,)), ((), ())), preferred_element_type=jnp.float32
    ).astype(jnp.bfloat16)
    cross_gate = jnp.dot(low_rank, cross_up, preferred_element_type=jnp.float32) + cross_bias
    base_wide = cross_base.astype(jnp.float32)
    crossed = base_wide * cross_gate + base_wide
    logits = jnp.dot(crossed, out_weight, precision=lax.Precision.HIGHEST)
    logit_grad = jax.nn.sigmoid(logits) - labels_dev.astype(jnp.float32)
    grad_crossed = logit_grad[:, None] * out_weight[None, :]
    g_cross = (grad_crossed * base_wide).astype(jnp.bfloat16)
    g_low = lax.dot_general(
        g_cross, cross_up, (((1,), (1,)), ((), ())), preferred_element_type=jnp.float32
    ).astype(jnp.bfloat16)
    up_part = lax.dot_general(
        low_rank, g_cross, (((0,), (0,)), ((), ())), preferred_element_type=jnp.float32
    )
    down_part = lax.dot_general(
        g_low, cross_base, (((0,), (0,)), ((), ())), preferred_element_type=jnp.float32
    )
    grad_base = grad_crossed * (cross_gate + 1.0) + jnp.dot(
        g_low, cross_down, preferred_element_type=jnp.float32
    )
    grad_pooled = grad_base[:, width:].reshape(batch, -1, width)
    contrib = bag_coef[..., None] * grad_pooled[:, :, None, :]
    cache_grad = (
        jnp.zeros(cached_rows.shape, jnp.float32)
        .at[ids_dev.reshape(-1)]
        .add(contrib.reshape(-1, width))
    )
    return (up_part, down_part, cache_grad)


def plain_local(
    emb_table,
    cross_up,
    cross_down,
    cross_bias,
    out_weight,
    bottom_weight,
    bottom_bias,
    dense_in,
    labels,
    lookup_ids,
    bag_weight,
    bag_length,
    want_blocks,
    hot_blocks,
    hot_count,
):
    owners = lax.axis_size("table")
    blocks = emb_table.reshape(-1, BLOCK, EMB)
    block_total = blocks.shape[0]
    wanted = want_blocks.reshape(owners, want_blocks.shape[3])
    asked_for = lax.all_to_all(wanted, "table", split_axis=0, concat_axis=0, tiled=True)
    flat = emb_table.reshape(block_total, -1)
    numbers = jnp.arange(block_total, dtype=jnp.int32)

    def take(ids):
        pick = (ids.reshape(-1)[:, None] == numbers[None, :]).astype(jnp.bfloat16)
        rows = jnp.dot(pick, flat, preferred_element_type=jnp.float32).astype(jnp.bfloat16)
        return rows.reshape(ids.shape + (BLOCK, EMB))

    served = take(asked_for)
    cold_rows = lax.all_to_all(served, "table", split_axis=0, concat_axis=0, tiled=True)
    slot_count = hot_blocks.shape[1]
    alive = jnp.arange(slot_count, dtype=jnp.int32) < hot_count[0]
    own_hot = jnp.where(alive[:, None, None], take(hot_blocks[0]), jnp.zeros((), jnp.bfloat16))
    hot_rows = lax.all_gather(own_hot[:, None], "table", axis=1, tiled=True)
    cold_count = cold_rows.shape[0] * cold_rows.shape[1] * BLOCK
    cached_rows = jnp.concatenate([cold_rows.reshape(-1, EMB), hot_rows.reshape(-1, EMB)], 0)
    up_part, down_part, cache_grad = local_step(
        cached_rows,
        dense_in,
        labels,
        lookup_ids,
        bag_weight,
        bag_length,
        cross_up,
        cross_down,
        cross_bias,
        out_weight,
        bottom_weight,
        bottom_bias,
    )
    cold_grad = cache_grad[:cold_count].reshape(cold_rows.shape).astype(jnp.bfloat16)
    returned = lax.all_to_all(cold_grad, "table", split_axis=0, concat_axis=0, tiled=True)
    hot_grad = cache_grad[cold_count:].reshape(hot_rows.shape)
    hot_sums = lax.psum_scatter(hot_grad, "table", scatter_dimension=1, tiled=True)[:, 0]
    block_ids = jnp.arange(block_total, dtype=jnp.int32)
    cold_pick = (asked_for.reshape(-1)[:, None] == block_ids[None, :]).astype(jnp.bfloat16)
    hot_pick = ((hot_blocks[0][:, None] == block_ids[None, :]) & alive[:, None]).astype(jnp.float32)
    block_grad = lax.dot_general(
        cold_pick,
        returned.reshape(cold_pick.shape[0], -1),
        (((0,), (0,)), ((), ())),
        preferred_element_type=jnp.float32,
    )
    block_grad = block_grad + lax.dot_general(
        hot_pick,
        hot_sums.reshape(slot_count, -1),
        (((0,), (0,)), ((), ())),
        precision=lax.Precision.HIGHEST,
    )
    table_grad = lax.psum_scatter(
        block_grad.reshape(-1, EMB), "replica", scatter_dimension=0, tiled=True
    )
    up_grad, down_grad = (
        lax.psum_scatter(up_part, ("table", "replica"), scatter_dimension=0, tiled=True),
        lax.psum_scatter(down_part, ("table", "replica"), scatter_dimension=0, tiled=True),
    )
    return (up_grad, down_grad, table_grad)


def choose(mesh, *args):
    devices = mesh.shape["table"] * mesh.shape["replica"]
    powers = all(n > 1 and n & (n - 1) == 0 for n in mesh.shape.values())
    rank, width = args[1].shape
    ids, want, hot = args[9], args[12], args[13]
    cache = mesh.shape["table"] * (want.shape[3] + hot.shape[1]) * BLOCK
    picked = 2 * ids.shape[0] * ids.shape[1] * cache
    whole_tiles = rank % (devices * SUBLANES) == 0 and width % (PARTS * LANES) == 0
    if powers and whole_tiles and ids.shape[0] == LANES and picked < 2**23:
        return fast_local(*args)
    return plain_local(*args)


def solution(mesh):
    local = functools.partial(choose, mesh)
    placed = (
        P("table", None),
        P(),
        P(),
        P(),
        P(),
        P(),
        P(),
        P(("table", "replica"), None),
        P(("table", "replica")),
        P(("table", "replica"), None, None),
        P(("table", "replica"), None, None),
        P(("table", "replica"), None),
        P("table", "replica", None, None),
        P("table", None),
        P("table"),
    )
    return jax.shard_map(
        local,
        mesh=mesh,
        in_specs=placed,
        out_specs=(
            P(("table", "replica"), None),
            P(("table", "replica"), None),
            P(("table", "replica"), None),
        ),
        check_vma=False,
    )
```

```python
import functools

import jax
import jax.numpy as jnp
from jax import lax
from jax.experimental import pallas as pl
from jax.experimental.pallas import tpu as pltpu
from jax.sharding import PartitionSpec as P

EMB = 128
BLOCK = 32
LANES = 128
SUBLANES = 8
MESH = pl.DeviceIdType.MESH
CHUNKS = 3
PARTS = 9
EARLY = 1
SHARE, FORWARD, FINISH = (1, 8), (2, 8), (3, 6)
HOT_AFTER = (5, 2, 0, 0)
F32 = jnp.float32
BF16 = jnp.bfloat16


def vmem(n):
    return [pl.BlockSpec(memory_space=pltpu.VMEM)] * n


def pick_rows(ids, emb_ref):
    found = [jnp.zeros((BLOCK, EMB), F32) for _ in ids]
    for b in range(emb_ref.shape[0] // BLOCK):
        block = emb_ref[b * BLOCK:(b + 1) * BLOCK, :].astype(F32)
        found = [jnp.where(i == b, block, f) for i, f in zip(ids, found)]
    return [f.astype(BF16) for f in found]


def whole_kernel(
    plan, stages, n_table, n_rep, buffers,
    want_ref, hot_ids_ref, count_ref, emb_hbm, ids_hbm, weight_hbm, length_hbm, dense_hbm,
    label_hbm, up_hbm, down_hbm, bias_hbm, outw_hbm, bw_hbm, bb_hbm,
    up_out, down_out, table_out,
    emb_ref, ids_ref, weight_ref, length_ref, dense_ref, label_ref, up_ref, down_ref,
    bias_ref, outw_ref, bw_ref, bb_ref, want_v, ask, serve, own_hot, cold_in, hot_in,
    pick, pick_low, base, part_sum, bow, grad_t, ids_cols, coef_cols, turn,
    down_t, up_t, x_own, x_send, x_in, acc, acc_hot, hot_send, hot_recv, fold_send, fold_recv, hot_all,
    hot_there, tg_cold, ag_cold, ag_ids,
    *rest,
):
    sends = rest[:buffers]
    recvs = rest[buffers:2 * buffers]
    (load_sem, id_send, id_recv, hs_send, hs_recv, cs_send, cs_recv, b_send, b_recv,
     w_send, w_recv, c_send, c_recv, a_send, a_recv, i_send, i_recv, f_send, f_recv,
     g_send, g_recv, m_send, m_recv) = rest[2 * buffers:]
    t = lax.axis_index("table")
    r = lax.axis_index("replica")
    wants = serve.shape[1]
    slots = own_hot.shape[0]
    feats, batch, cache = pick.shape
    bag = ids_ref.shape[1]
    width = base.shape[1]
    group = 16
    core = lax.rem(r, 2)
    mate = (t, r + 1 - 2 * core)

    def table_peer(k):
        return (lax.rem(t + k, n_table), r)

    def rep_peer(k):
        return (t, lax.rem(r + k, n_rep))

    def remote(src, dst, send, recv, device):
        return pltpu.make_async_remote_copy(
            src_ref=src, dst_ref=dst, send_sem=send, recv_sem=recv,
            device_id=device, device_id_type=MESH,
        )

    barrier = pltpu.get_barrier_semaphore()
    for k in range(1, n_table):
        pl.semaphore_signal(barrier, inc=1, device_id=table_peer(k), device_id_type=MESH)
    for k in range(1, n_rep):
        pl.semaphore_signal(barrier, inc=1, device_id=rep_peer(k), device_id_type=MESH)
    loads = [
        pltpu.make_async_copy(src, dst, load_sem.at[i])
        for i, (src, dst) in enumerate((
            (emb_hbm, emb_ref), (ids_hbm, ids_ref), (weight_hbm, weight_ref),
            (length_hbm, length_ref), (dense_hbm, dense_ref), (label_hbm, label_ref),
            (bw_hbm, bw_ref), (bb_hbm, bb_ref), (bias_hbm, bias_ref), (outw_hbm, outw_ref),
            (down_hbm, down_ref), (up_hbm, up_ref),
        ))
    ]
    for c in loads:
        c.start()
    for p in range(n_table):
        for w in range(wants):
            want_v[p, w:w + 1] = jnp.full((1, LANES), want_ref[0, 0, w, p], jnp.int32)
    ask[t] = want_v[t]
    hot_rows = []
    for s in range(slots):
        block = jnp.where(s < count_ref[0], hot_ids_ref[0, s], -1)
        hot_rows.append(jnp.full((1, LANES), block, jnp.int32))

    loads[0].wait()
    for s, rows in enumerate(pick_rows(hot_rows, emb_ref)):
        own_hot[s] = rows
    half_block = pl.ds(pl.multiple_of(core * (BLOCK // 2), BLOCK // 2), BLOCK // 2)
    hot_in[:, t, half_block] = own_hot[:, half_block]
    for c in loads[1:10]:
        c.wait()
    turn[...] = jnp.zeros_like(turn)
    for f in range(feats):
        turn[f * bag:(f + 1) * bag, :] = ids_ref[f].astype(F32)
    ids_cols[...] = turn[...].T
    spot = lax.broadcasted_iota(jnp.int32, (bag, batch), 0)
    for f in range(feats):
        live = spot < length_ref[f:f + 1, :]
        turn[f * bag:(f + 1) * bag, :] = jnp.where(live, weight_ref[f], 0.0)
    coef_cols[...] = turn[...].T

    def build_group(g):
        at = pl.ds(pl.multiple_of(g * group, group), group)
        ids = ids_cols[at, :]
        coef = coef_cols[at, :]
        lane = lax.broadcasted_iota(jnp.int32, (group, cache), 1).astype(F32)
        for f in range(feats):
            total = None
            for l in range(bag):
                j = f * bag + l
                term = jnp.where(ids[:, j:j + 1] == lane, coef[:, j:j + 1], 0.0)
                total = term if total is None else total + term
            high = total.astype(BF16)
            pick[f, at, :] = high
            pick_low[f, at, :] = (total - high.astype(F32)).astype(BF16)

    def build(first, last):
        @pl.loop(first, last)
        def _(g):
            build_group(g)

    build(0, EARLY)
    pl.semaphore_wait(barrier, n_table - 1 + n_rep - 1)

    id_copies = [
        remote(want_v.at[table_peer(k)[0]], ask.at[t], id_send.at[k], id_recv.at[k], table_peer(k))
        for k in range(1, n_table)
    ]
    hot_copies = [
        remote(own_hot.at[:, half_block], hot_in.at[:, t, half_block], hs_send.at[k],
               hs_recv.at[k], table_peer(k))
        for k in range(1, n_table)
    ]
    for c in id_copies + hot_copies:
        c.start()

    groups = batch // group
    first = groups * 3 // 4
    build(EARLY, first)
    for c in id_copies:
        c.wait()
    asked = [ask[p, w:w + 1, :] for p in range(n_table) for w in range(wants)]
    for i, rows in enumerate(pick_rows(asked, emb_ref)):
        serve[i // wants, i % wants] = rows
    cold_copies = [
        remote(serve.at[table_peer(k)[0]], cold_in.at[t], cs_send.at[k], cs_recv.at[k],
               table_peer(k))
        for k in range(1, n_table)
    ]
    for c in cold_copies:
        c.start()
    for c in hot_copies:
        c.wait()
    hot_mate = remote(
        hot_in.at[:, :, half_block], hot_in.at[:, :, half_block], m_send.at[0], m_recv.at[0], mate
    )
    hot_mate.start()
    cold_in[t] = serve[t]
    ag_ids[r] = ask[...]
    id_shares = [
        remote(ask, ag_ids.at[r], i_send.at[k], i_recv.at[k], rep_peer(k)) for k in range(1, n_rep)
    ]
    for c in id_shares:
        c.start()
    second = groups * 3 // 4
    build(first, second)

    bottom = jnp.zeros((batch, EMB), F32) + bb_ref[...]
    features = dense_ref.shape[0]
    turn[0:features, :] = dense_ref[...]
    turn[features:features + 1, :] = label_ref[...].astype(F32)
    dense = turn[...].T
    label = dense[:, features:features + 1]
    for j in range(features):
        bottom = bottom + dense[:, j:j + 1] * bw_ref[j:j + 1, :]
    lsum = jnp.zeros((batch, LANES), F32)

    def settle(lsum, j, value):
        cols = slice(j * EMB, (j + 1) * EMB)
        b = value.astype(BF16)
        base[0:batch, cols] = b
        x = b.astype(F32) * outw_ref[cols].reshape(1, -1)
        bow[:, cols] = x.astype(BF16)
        return lsum + x * (bias_ref[cols].reshape(1, -1) + 1.0)

    lsum = settle(lsum, 0, jnp.maximum(bottom, 0.0))
    cold = n_table * wants * BLOCK
    some = 2 if feats % 2 == 0 else 1

    def pool(f, cols, rows):
        at = slice(f, f + some)
        return jnp.dot(
            pick[at, :, cols].reshape(some * batch, -1), rows, preferred_element_type=F32
        ) + jnp.dot(
            pick_low[at, :, cols].reshape(some * batch, -1), rows, preferred_element_type=F32
        )

    def pool_hot(start, count, rows):
        at = pl.ds(start, count)
        many = max(2 * batch // count, 1)
        for f in range(0, feats, many):
            to = min(f + many, feats)
            m = (to - f) * count
            pooled = jnp.dot(
                pick[f:to, at, cold:].reshape(m, -1), rows, preferred_element_type=F32
            ) + jnp.dot(
                pick_low[f:to, at, cold:].reshape(m, -1), rows, preferred_element_type=F32
            )
            for i in range(to - f):
                part_sum[at, (f + i) * EMB:(f + i + 1) * EMB] = pooled[i * count:(i + 1) * count]

    def turn_weights(n):
        for i in range(width // EMB // CHUNKS):
            cols = pl.ds(pl.multiple_of(n * (width // CHUNKS) + i * EMB, EMB), EMB)
            down_t[cols, :] = down_ref[:, cols].T
            up_t[cols, :] = up_ref[:, cols].T

    for c in loads[10:]:
        c.wait()
    hot_mate.wait()
    steps = groups - second
    each = second // steps * group

    @pl.loop(0, steps)
    def _(j):
        rows = hot_in[...].reshape(cache - cold, EMB)
        pool_hot(pl.multiple_of(j * each, group), each, rows)
        turn_weights(j)
        build_group(second + j)

    done = steps * each
    pool_hot(done, batch - done, hot_in[...].reshape(cache - cold, EMB))
    for n in range(steps, CHUNKS):
        turn_weights(n)
    for c in cold_copies:
        c.wait()
    rows = cold_in[...].reshape(cold, EMB)
    wide = width // CHUNKS
    base_copies = []
    for f in range(0, feats, some):
        pooled = pool(f, slice(0, cold), rows)
        for i in range(some):
            before = part_sum[:, (f + i) * EMB:(f + i + 1) * EMB]
            lsum = settle(lsum, f + i + 1, pooled[i * batch:(i + 1) * batch] + before)
        n = len(base_copies)
        while n < CHUNKS and (f + some + 1) * EMB >= (n + 1) * wide:
            cols = slice(n * wide, (n + 1) * wide)
            base_copies.append(remote(
                base.at[0:batch, cols], base.at[batch:2 * batch, cols], b_send.at[n],
                b_recv.at[n], mate,
            ))
            base_copies[n].start()
            n += 1

    low = jnp.dot(base[0:batch], down_t[...], preferred_element_type=F32)
    high = jnp.dot(bow[...], up_t[...], preferred_element_type=F32)
    low_b = low.astype(BF16)
    prod = low_b.astype(F32) * high
    rank = prod.shape[1]
    for i in range(rank // LANES):
        lsum = lsum + prod[:, i * LANES:(i + 1) * LANES]
    logit = jnp.sum(lsum, axis=1, keepdims=True)
    lgrad = jax.nn.sigmoid(logit) - label
    g_low_f = high * lgrad
    g_low = g_low_f.astype(BF16)
    chips, two = acc.shape[0], acc.shape[1]
    own = two // 2
    turned = jnp.concatenate([low * lgrad, g_low_f], axis=1).T
    turned = turned.reshape(2, chips, 2, own, batch)
    is_first = core == 0
    mine = jnp.where(is_first, turned[:, :, 0], turned[:, :, 1])
    other = jnp.where(is_first, turned[:, :, 1], turned[:, :, 0])
    x_send[...] = other.reshape(rank, batch).astype(BF16)
    x_copy = remote(x_send, x_in, m_send.at[1], m_recv.at[1], mate)
    x_copy.start()
    x_own[...] = mine.reshape(rank, batch).astype(BF16)

    def bit_of(axis, bit):
        return lax.rem((t if axis == "table" else r) // (1 << bit), 2)

    def partner(axis, bit):
        shift = (1 - 2 * bit_of(axis, bit)) * (1 << bit)
        return (t + shift, r) if axis == "table" else (t, r + shift)

    parts = len(plan)
    step = width // parts
    lows = [0] * parts
    sizes = [chips] * parts
    copies = {}
    deep = len(stages[0])

    def launch(p, s):
        axis, bit = stages[p][s]
        at_bit = bit_of(axis, bit)
        half = sizes[p] // 2
        keep = lows[p] + at_bit * half
        give = lows[p] + (1 - at_bit) * half
        cols = slice(p * step, (p + 1) * step)
        i = p * deep + s
        sends[i][...] = acc[pl.ds(give, half), :, cols].astype(BF16)
        copies[p, s] = remote(sends[i], recvs[i], w_send.at[i], w_recv.at[i], partner(axis, bit))
        copies[p, s].start()
        lows[p], sizes[p] = keep, half

    def absorb(p, s):
        copies[p, s].wait()
        i = p * deep + s
        cols = slice(p * step, (p + 1) * step)
        at = pl.ds(lows[p], sizes[p])
        total = acc[at, :, cols] + recvs[i][...].astype(F32)
        if s + 1 < deep:
            acc[at, :, cols] = total
        else:
            up_out[:, cols] = total[0, 0:own]
            down_out[:, cols] = total[0, own:]

    for c in base_copies:
        c.wait()
    x_copy.wait()
    factors = jnp.concatenate([x_own[...], x_in[...]], axis=1)
    for c in range(CHUNKS):
        at = slice(c * wide, (c + 1) * wide)
        both = jnp.dot(factors, base[:, at], preferred_element_type=F32)
        up = both[0:rank // 2] * outw_ref[at].reshape(1, -1)
        down = both[rank // 2:]
        for i in range(parts // CHUNKS):
            p = c * (parts // CHUNKS) + i
            part, cols = slice(i * step, (i + 1) * step), slice(p * step, (p + 1) * step)
            for d in range(chips):
                rows_d = slice(d * own, (d + 1) * own)
                acc[plan[p][d], 0:own, cols] = up[rows_d, part]
                acc[plan[p][d], own:two, cols] = down[rows_d, part]
            launch(p, 0)

    for c in range(CHUNKS):
        at = slice(c * wide, (c + 1) * wide)
        gate = jnp.dot(low_b, up_ref[:, at], preferred_element_type=F32)
        gate = gate + (bias_ref[at].reshape(1, -1) + 1.0)
        grad = (lgrad * outw_ref[at].reshape(1, -1)) * gate + jnp.dot(
            g_low, down_ref[:, at], preferred_element_type=F32
        )
        for i in range(wide // LANES):
            f = (c * wide) // LANES + i - 1
            if f >= 0:
                grad_t[:, f * batch:(f + 1) * batch] = (
                    grad[:, i * LANES:(i + 1) * LANES].T.astype(BF16)
                )
    total = jnp.dot(
        grad_t[...], pick[...].reshape(feats * batch, cache), preferred_element_type=F32
    ).T
    tg_cold[...] = total[:cold].astype(BF16).reshape(tg_cold.shape)
    out_copies = []
    for k in range(1, n_table):
        to = table_peer(k)
        out_copies.append(
            remote(tg_cold.at[to[0]], ag_cold.at[r, t], c_send.at[k], c_recv.at[k], to)
        )
    for c in out_copies:
        c.start()
    ag_cold[r, t] = tg_cold[t]
    halves = total[cold:].reshape(slots, n_table, 2, BLOCK // 2, EMB)
    other = jnp.where(is_first, halves[:, :, 1], halves[:, :, 0])
    mine = jnp.where(is_first, halves[:, :, 0], halves[:, :, 1])
    folds = n_table.bit_length() - 1
    for o in range(n_table):
        at = sum(((o >> b) & 1) << (folds - 1 - b) for b in range(folds))
        for s in range(slots):
            hot_send[at, s] = other[s, o].astype(BF16)
            acc_hot[at, s] = mine[s, o]
    hot_pair = remote(hot_send, hot_recv, m_send.at[2], m_recv.at[2], mate)
    hot_pair.start()
    hot_at = [0, n_table]
    hot_copies = []

    def hot_launch():
        b = len(hot_copies)
        half = hot_at[1] // 2
        at_bit = bit_of("table", b)
        keep, give = hot_at[0] + at_bit * half, hot_at[0] + (1 - at_bit) * half
        span = pl.ds(n_table - 2 * half, half)
        fold_send[span] = acc_hot[pl.ds(give, half)].astype(BF16)
        hot_copies.append(remote(
            fold_send.at[span], fold_recv.at[span], f_send.at[b], f_recv.at[b],
            partner("table", b),
        ))
        hot_copies[b].start()
        hot_at[:] = [keep, half]

    def hot_absorb():
        hot_copies[-1].wait()
        at, half = pl.ds(hot_at[0], hot_at[1]), hot_at[1]
        span = slice(n_table - 2 * half, n_table - half)
        acc_hot[at] = acc_hot[at] + fold_recv[span].astype(F32)

    rep_bits = n_rep.bit_length() - 1
    hot_shares = []

    def hot_step(n):
        if n < folds:
            hot_absorb()
            if n + 1 < folds:
                hot_launch()
            else:
                hot_all[0] = acc_hot[hot_at[0]]
        elif n < folds + rep_bits - 1:
            hot_shares[-1].wait()
            k = n - folds
            hot_all[k + 1] = hot_all[k] + hot_there[k]
        k = n - folds + 1
        if 0 <= k < rep_bits:
            to = partner("replica", k + 1) if k + 1 < rep_bits else mate
            hot_shares.append(
                remote(hot_all.at[k], hot_there.at[k], g_send.at[k], g_recv.at[k], to)
            )
            hot_shares[k].start()

    hot_pair.wait()
    acc_hot[...] = acc_hot[...] + hot_recv[...].astype(F32)
    hot_launch()

    across = (t, lax.rem(r + n_rep // 2, n_rep))
    shares = []

    def share():
        for c in out_copies:
            c.wait()
        for n, to in enumerate((across, mate)):
            shares.append(remote(ag_cold.at[r], ag_cold.at[r], a_send.at[n], a_recv.at[n], to))
            shares[n].start()

    def forward():
        shares[0].wait()
        there = lax.rem(r + n_rep // 2, n_rep)
        shares.append(
            remote(ag_cold.at[there], ag_cold.at[there], a_send.at[2], a_recv.at[2], mate)
        )
        shares[2].start()

    mine_blocks = table_out.shape[0]
    first_block = r * mine_blocks

    def finish_cold():
        for c in id_shares:
            c.wait()
        shares[1].wait()
        shares[2].wait()
        total = [jnp.zeros((BLOCK, EMB), F32) for _ in range(mine_blocks)]
        for q in range(n_rep):
            for o in range(n_table):
                for w in range(wants):
                    ids = ag_ids[q, o, w:w + 1, :] - first_block
                    val = ag_cold[q, o, w].astype(F32)
                    for b in range(mine_blocks):
                        total[b] = total[b] + jnp.where(ids == b, val, 0.0)
        for b in range(mine_blocks):
            table_out[b] = total[b]

    def finish_hot():
        hot_shares[-1].wait()
        ours, theirs = hot_all[rep_bits - 1], hot_there[rep_bits - 1]
        for b in range(mine_blocks):
            total = table_out[b]
            for h in range(slots):
                ids = jnp.where(hot_rows[h] >= 0, hot_rows[h] - first_block, -1)
                val = jnp.concatenate([
                    jnp.where(is_first, ours[h], theirs[h]), jnp.where(is_first, theirs[h], ours[h])
                ], axis=0)
                total = total + jnp.where(ids == b, val, 0.0)
            table_out[b] = total

    hot_steps = list(range(folds + rep_bits - 1))
    for s in range(deep):
        for p in range(parts):
            absorb(p, s)
            if s + 1 < deep:
                launch(p, s + 1)
            if hot_steps and p == HOT_AFTER[min(s, len(HOT_AFTER) - 1)]:
                hot_step(hot_steps.pop(0))
            if (s, p) == SHARE:
                share()
            if (s, p) == FORWARD:
                forward()
            if (s, p) == FINISH:
                finish_cold()
    while hot_steps:
        hot_step(hot_steps.pop(0))
    finish_hot()


def whole(
    plan, stages, n_table, n_rep, want, hot_ids, count, emb, ids, weight, length, dense, labels,
    up, down, bias, outw, bw, bb,
):
    feats, bag, batch = ids.shape
    padded = -(-feats * bag // LANES) * LANES
    devices = n_table * n_rep
    rank, width = up.shape
    own = rank // devices
    two, chips = 2 * own, devices // 2
    wants, slots = want.shape[2], hot_ids.shape[1]
    cache = n_table * (wants + slots) * BLOCK
    step = width // PARTS
    mine = emb.shape[0] // BLOCK // n_rep
    shapes = []
    for part in stages:
        size = chips
        for _ in part:
            size //= 2
            shapes.append(pltpu.VMEM((size, two, step), BF16))
    dma = pltpu.SemaphoreType.DMA
    one, many = pl.BlockSpec(memory_space=pltpu.SMEM), pl.BlockSpec(memory_space=pltpu.HBM)
    return pl.pallas_call(
        functools.partial(whole_kernel, plan, stages, n_table, n_rep, len(shapes)),
        out_shape=[
            pltpu.VMEM((own, width), F32),
            pltpu.VMEM((own, width), F32),
            pltpu.VMEM((mine, BLOCK, EMB), F32),
        ],
        in_specs=[one] * 3 + [many] * 12,
        out_specs=vmem(3),
        scratch_shapes=[
            pltpu.VMEM(a.shape, a.dtype)
            for a in (emb, ids, weight, length, dense, labels, up, down, bias, outw, bw, bb)
        ] + [
            pltpu.VMEM((n_table, wants, LANES), jnp.int32),
            pltpu.VMEM((n_table, wants, LANES), jnp.int32),
            pltpu.VMEM((n_table, wants, BLOCK, EMB), BF16),
            pltpu.VMEM((slots, BLOCK, EMB), BF16),
            pltpu.VMEM((n_table, wants, BLOCK, EMB), BF16),
            pltpu.VMEM((slots, n_table, BLOCK, EMB), BF16),
            pltpu.VMEM((feats, batch, cache), BF16),
            pltpu.VMEM((feats, batch, cache), BF16),
            pltpu.VMEM((2 * batch, width), BF16),
            pltpu.VMEM((batch, width), F32),
            pltpu.VMEM((batch, width), BF16),
            pltpu.VMEM((EMB, feats * batch), BF16),
            pltpu.VMEM((batch, padded), F32),
            pltpu.VMEM((batch, padded), F32),
            pltpu.VMEM((padded, batch), F32),
            pltpu.VMEM((width, rank), BF16),
            pltpu.VMEM((width, rank), BF16),
            pltpu.VMEM((rank, batch), BF16),
            pltpu.VMEM((rank, batch), BF16),
            pltpu.VMEM((rank, batch), BF16),
            pltpu.VMEM((chips, two, width), F32),
            pltpu.VMEM((n_table, slots, BLOCK // 2, EMB), F32),
        ] + [pltpu.VMEM((n_table, slots, BLOCK // 2, EMB), BF16)] * 4 + [
            pltpu.VMEM((n_rep.bit_length() - 1, slots, BLOCK // 2, EMB), F32),
            pltpu.VMEM((n_rep.bit_length() - 1, slots, BLOCK // 2, EMB), F32),
            pltpu.VMEM((n_table, wants, BLOCK, EMB), BF16),
            pltpu.VMEM((n_rep, n_table, wants, BLOCK, EMB), BF16),
            pltpu.VMEM((n_rep, n_table, wants, LANES), jnp.int32),
        ] + shapes + shapes + [dma((12,))] + [dma((n_table,))] * 6 + [dma((CHUNKS,))] * 2
        + [dma((len(shapes),))] * 2 + [dma((n_table,))] * 2 + [dma((3,))] * 2
        + [dma((n_rep,))] * 2 + [dma((n_table,))] * 2 + [dma((n_rep,))] * 2 + [dma((3,))] * 2,
        compiler_params=pltpu.CompilerParams(
            collective_id=0, has_side_effects=True, vmem_limit_bytes=60 * 2**20
        ),
        name="whole",
    )(want, hot_ids, count, emb, ids, weight, length, dense, labels, up, down, bias, outw, bw, bb)


def finish_kernel(*refs):
    n = len(refs) // 2
    sem = refs[-1]
    copies = [
        pltpu.make_async_copy(refs[i], refs[n + i], sem.at[i]) for i in range(n)
    ]
    for c in copies:
        c.start()
    for c in copies:
        c.wait()


def finish(*arrays):
    many = [pl.BlockSpec(memory_space=pltpu.VMEM)] * len(arrays)
    outs = [pl.BlockSpec(memory_space=pltpu.HBM)] * len(arrays)
    return pl.pallas_call(
        finish_kernel,
        out_shape=[jax.ShapeDtypeStruct(a.shape, a.dtype) for a in arrays],
        in_specs=many,
        out_specs=outs,
        scratch_shapes=[pltpu.SemaphoreType.DMA((len(arrays),))],
        name="finish",
    )(*arrays)


def make_stages(n_table, n_rep, parts):
    rep = [("replica", b) for b in range(1, n_rep.bit_length() - 1)]
    tab = [("table", b) for b in range(n_table.bit_length() - 1)]
    bits = rep + tab
    tail = bits[:-1]
    turned = [tail[p % len(tail):] + tail[:p % len(tail)] for p in range(parts)]
    swapped = [p % 3 == 0 for p in range(parts)]
    return [
        part[:-1] + bits[-1:] + part[-1:] if swap else part + bits[-1:]
        for part, swap in zip(turned, swapped)
    ]


def places(stages, n_rep, chips):
    plan = []
    pairs = n_rep // 2
    for part in stages:
        row = []
        for d in range(chips):
            at = 0
            for axis, bit in part:
                number = d // pairs if axis == "table" else (d % pairs) * 2
                at = at * 2 + (number >> bit) % 2
            row.append(at)
        plan.append(row)
    return plan


def fast_local(
    emb_table, cross_up, cross_down, cross_bias, out_weight, bottom_weight, bottom_bias,
    dense_in, labels, lookup_ids, bag_weight, bag_length, want_blocks, hot_blocks, hot_count,
):
    owners, reps = lax.axis_size("table"), lax.axis_size("replica")
    stages = make_stages(owners, reps, PARTS)
    plan = places(stages, reps, owners * reps // 2)
    up, down, table = whole(
        plan, stages, owners, reps, want_blocks.transpose(0, 1, 3, 2), hot_blocks, hot_count, emb_table,
        lookup_ids.transpose(1, 2, 0), bag_weight.transpose(1, 2, 0), bag_length.T,
        dense_in.T, labels[None], cross_up, cross_down, cross_bias, out_weight,
        bottom_weight, bottom_bias[None],
    )
    up, down, table = [pltpu.with_memory_space_constraint(a, pltpu.VMEM) for a in (up, down, table)]
    u, d, t = finish(up, down, table)
    return u, d, t.reshape(-1, EMB)


def local_step(
    cached_rows,
    dense_dev,
    labels_dev,
    ids_dev,
    weight_dev,
    length_dev,
    cross_up,
    cross_down,
    cross_bias,
    out_weight,
    bottom_weight,
    bottom_bias,
):
    batch = ids_dev.shape[0]
    width = cached_rows.shape[1]
    gathered = cached_rows[ids_dev].astype(jnp.float32)
    slots = jnp.arange(ids_dev.shape[2], dtype=jnp.int32)
    bag_coef = jnp.where(
        slots[None, None, :] < length_dev[:, :, None], weight_dev, jnp.zeros((), jnp.float32)
    )
    pooled = jnp.sum(bag_coef[..., None] * gathered, axis=2)
    bottom = jax.nn.relu(
        jnp.dot(dense_dev, bottom_weight, precision=lax.Precision.HIGHEST) + bottom_bias
    )
    cross_base = jnp.concatenate([bottom, pooled.reshape(batch, -1)], 1).astype(jnp.bfloat16)
    low_rank = lax.dot_general(
        cross_base, cross_down, (((1,), (1,)), ((), ())), preferred_element_type=jnp.float32
    ).astype(jnp.bfloat16)
    cross_gate = jnp.dot(low_rank, cross_up, preferred_element_type=jnp.float32) + cross_bias
    base_wide = cross_base.astype(jnp.float32)
    crossed = base_wide * cross_gate + base_wide
    logits = jnp.dot(crossed, out_weight, precision=lax.Precision.HIGHEST)
    logit_grad = jax.nn.sigmoid(logits) - labels_dev.astype(jnp.float32)
    grad_crossed = logit_grad[:, None] * out_weight[None, :]
    g_cross = (grad_crossed * base_wide).astype(jnp.bfloat16)
    g_low = lax.dot_general(
        g_cross, cross_up, (((1,), (1,)), ((), ())), preferred_element_type=jnp.float32
    ).astype(jnp.bfloat16)
    up_part = lax.dot_general(
        low_rank, g_cross, (((0,), (0,)), ((), ())), preferred_element_type=jnp.float32
    )
    down_part = lax.dot_general(
        g_low, cross_base, (((0,), (0,)), ((), ())), preferred_element_type=jnp.float32
    )
    grad_base = grad_crossed * (cross_gate + 1.0) + jnp.dot(
        g_low, cross_down, preferred_element_type=jnp.float32
    )
    grad_pooled = grad_base[:, width:].reshape(batch, -1, width)
    contrib = bag_coef[..., None] * grad_pooled[:, :, None, :]
    cache_grad = (
        jnp.zeros(cached_rows.shape, jnp.float32)
        .at[ids_dev.reshape(-1)]
        .add(contrib.reshape(-1, width))
    )
    return (up_part, down_part, cache_grad)


def plain_local(
    emb_table,
    cross_up,
    cross_down,
    cross_bias,
    out_weight,
    bottom_weight,
    bottom_bias,
    dense_in,
    labels,
    lookup_ids,
    bag_weight,
    bag_length,
    want_blocks,
    hot_blocks,
    hot_count,
):
    owners = lax.axis_size("table")
    blocks = emb_table.reshape(-1, BLOCK, EMB)
    block_total = blocks.shape[0]
    wanted = want_blocks.reshape(owners, want_blocks.shape[3])
    asked_for = lax.all_to_all(wanted, "table", split_axis=0, concat_axis=0, tiled=True)
    flat = emb_table.reshape(block_total, -1)
    numbers = jnp.arange(block_total, dtype=jnp.int32)

    def take(ids):
        pick = (ids.reshape(-1)[:, None] == numbers[None, :]).astype(jnp.bfloat16)
        rows = jnp.dot(pick, flat, preferred_element_type=jnp.float32).astype(jnp.bfloat16)
        return rows.reshape(ids.shape + (BLOCK, EMB))

    served = take(asked_for)
    cold_rows = lax.all_to_all(served, "table", split_axis=0, concat_axis=0, tiled=True)
    slot_count = hot_blocks.shape[1]
    alive = jnp.arange(slot_count, dtype=jnp.int32) < hot_count[0]
    own_hot = jnp.where(alive[:, None, None], take(hot_blocks[0]), jnp.zeros((), jnp.bfloat16))
    hot_rows = lax.all_gather(own_hot[:, None], "table", axis=1, tiled=True)
    cold_count = cold_rows.shape[0] * cold_rows.shape[1] * BLOCK
    cached_rows = jnp.concatenate([cold_rows.reshape(-1, EMB), hot_rows.reshape(-1, EMB)], 0)
    up_part, down_part, cache_grad = local_step(
        cached_rows,
        dense_in,
        labels,
        lookup_ids,
        bag_weight,
        bag_length,
        cross_up,
        cross_down,
        cross_bias,
        out_weight,
        bottom_weight,
        bottom_bias,
    )
    cold_grad = cache_grad[:cold_count].reshape(cold_rows.shape).astype(jnp.bfloat16)
    returned = lax.all_to_all(cold_grad, "table", split_axis=0, concat_axis=0, tiled=True)
    hot_grad = cache_grad[cold_count:].reshape(hot_rows.shape)
    hot_sums = lax.psum_scatter(hot_grad, "table", scatter_dimension=1, tiled=True)[:, 0]
    block_ids = jnp.arange(block_total, dtype=jnp.int32)
    cold_pick = (asked_for.reshape(-1)[:, None] == block_ids[None, :]).astype(jnp.bfloat16)
    hot_pick = ((hot_blocks[0][:, None] == block_ids[None, :]) & alive[:, None]).astype(jnp.float32)
    block_grad = lax.dot_general(
        cold_pick,
        returned.reshape(cold_pick.shape[0], -1),
        (((0,), (0,)), ((), ())),
        preferred_element_type=jnp.float32,
    )
    block_grad = block_grad + lax.dot_general(
        hot_pick,
        hot_sums.reshape(slot_count, -1),
        (((0,), (0,)), ((), ())),
        precision=lax.Precision.HIGHEST,
    )
    table_grad = lax.psum_scatter(
        block_grad.reshape(-1, EMB), "replica", scatter_dimension=0, tiled=True
    )
    up_grad, down_grad = (
        lax.psum_scatter(up_part, ("table", "replica"), scatter_dimension=0, tiled=True),
        lax.psum_scatter(down_part, ("table", "replica"), scatter_dimension=0, tiled=True),
    )
    return (up_grad, down_grad, table_grad)


def choose(mesh, *args):
    devices = mesh.shape["table"] * mesh.shape["replica"]
    powers = all(n > 1 and n & (n - 1) == 0 for n in mesh.shape.values())
    rank, width = args[1].shape
    ids, want, hot = args[9], args[12], args[13]
    cache = mesh.shape["table"] * (want.shape[3] + hot.shape[1]) * BLOCK
    picked = 2 * ids.shape[0] * ids.shape[1] * cache
    whole_tiles = rank % (devices * SUBLANES) == 0 and width % (PARTS * LANES) == 0
    if powers and whole_tiles and ids.shape[0] == LANES and picked < 2**23:
        return fast_local(*args)
    return plain_local(*args)


def solution(mesh):
    local = functools.partial(choose, mesh)
    placed = (
        P("table", None),
        P(),
        P(),
        P(),
        P(),
        P(),
        P(),
        P(("table", "replica"), None),
        P(("table", "replica")),
        P(("table", "replica"), None, None),
        P(("table", "replica"), None, None),
        P(("table", "replica"), None),
        P("table", "replica", None, None),
        P("table", None),
        P("table"),
    )
    return jax.shard_map(
        local,
        mesh=mesh,
        in_specs=placed,
        out_specs=(
            P(("table", "replica"), None),
            P(("table", "replica"), None),
            P(("table", "replica"), None),
        ),
        check_vma=False,
    )
```

```python
import functools

import jax
import jax.numpy as jnp
from jax import lax
from jax.experimental import pallas as pl
from jax.experimental.pallas import tpu as pltpu
from jax.sharding import PartitionSpec as P

EMB = 128
BLOCK = 32
LANES = 128
SUBLANES = 8
MESH = pl.DeviceIdType.MESH
CHUNKS = 3
PARTS = 9
EARLY = 1
SHARE, FORWARD, FINISH = (0, 8), (1, 8), (2, 8)
HOT_AFTER = (5, 2, 0, 0)
F32 = jnp.float32
BF16 = jnp.bfloat16


def vmem(n):
    return [pl.BlockSpec(memory_space=pltpu.VMEM)] * n


def pick_rows(ids, emb_ref):
    found = [jnp.zeros((BLOCK, EMB), F32) for _ in ids]
    for b in range(emb_ref.shape[0] // BLOCK):
        block = emb_ref[b * BLOCK:(b + 1) * BLOCK, :].astype(F32)
        found = [jnp.where(i == b, block, f) for i, f in zip(ids, found)]
    return [f.astype(BF16) for f in found]


def whole_kernel(
    plan, stages, n_table, n_rep, buffers,
    want_ref, hot_ids_ref, count_ref, emb_hbm, ids_hbm, weight_hbm, length_hbm, dense_hbm,
    label_hbm, up_hbm, down_hbm, bias_hbm, outw_hbm, bw_hbm, bb_hbm,
    up_out, down_out, table_out,
    emb_ref, ids_ref, weight_ref, length_ref, dense_ref, label_ref, up_ref, down_ref,
    bias_ref, outw_ref, bw_ref, bb_ref, want_v, ask, serve, own_hot, cold_in, hot_in,
    pick, pick_low, base, part_sum, bow, grad_t, ids_cols, coef_cols, turn,
    down_t, up_t, x_own, x_send, x_in, acc, acc_hot, hot_send, hot_recv, fold_send, fold_recv, hot_all,
    hot_there, tg_cold, ag_cold, ag_ids,
    *rest,
):
    sends = rest[:buffers]
    recvs = rest[buffers:2 * buffers]
    (load_sem, id_send, id_recv, hs_send, hs_recv, cs_send, cs_recv, b_send, b_recv,
     w_send, w_recv, c_send, c_recv, a_send, a_recv, i_send, i_recv, f_send, f_recv,
     g_send, g_recv, m_send, m_recv) = rest[2 * buffers:]
    t = lax.axis_index("table")
    r = lax.axis_index("replica")
    wants = serve.shape[1]
    slots = own_hot.shape[0]
    feats, batch, cache = pick.shape
    bag = ids_ref.shape[1]
    width = base.shape[1]
    group = 16
    core = lax.rem(r, 2)
    mate = (t, r + 1 - 2 * core)

    def table_peer(k):
        return (lax.rem(t + k, n_table), r)

    def rep_peer(k):
        return (t, lax.rem(r + k, n_rep))

    def remote(src, dst, send, recv, device):
        return pltpu.make_async_remote_copy(
            src_ref=src, dst_ref=dst, send_sem=send, recv_sem=recv,
            device_id=device, device_id_type=MESH,
        )

    barrier = pltpu.get_barrier_semaphore()
    for k in range(1, n_table):
        pl.semaphore_signal(barrier, inc=1, device_id=table_peer(k), device_id_type=MESH)
    for k in range(1, n_rep):
        pl.semaphore_signal(barrier, inc=1, device_id=rep_peer(k), device_id_type=MESH)
    loads = [
        pltpu.make_async_copy(src, dst, load_sem.at[i])
        for i, (src, dst) in enumerate((
            (emb_hbm, emb_ref), (ids_hbm, ids_ref), (weight_hbm, weight_ref),
            (length_hbm, length_ref), (dense_hbm, dense_ref), (label_hbm, label_ref),
            (bw_hbm, bw_ref), (bb_hbm, bb_ref), (bias_hbm, bias_ref), (outw_hbm, outw_ref),
            (down_hbm, down_ref), (up_hbm, up_ref),
        ))
    ]
    for c in loads:
        c.start()
    for p in range(n_table):
        for w in range(wants):
            want_v[p, w:w + 1] = jnp.full((1, LANES), want_ref[0, 0, w, p], jnp.int32)
    ask[t] = want_v[t]
    hot_rows = []
    for s in range(slots):
        block = jnp.where(s < count_ref[0], hot_ids_ref[0, s], -1)
        hot_rows.append(jnp.full((1, LANES), block, jnp.int32))

    loads[0].wait()
    for s, rows in enumerate(pick_rows(hot_rows, emb_ref)):
        own_hot[s] = rows
    half_block = pl.ds(pl.multiple_of(core * (BLOCK // 2), BLOCK // 2), BLOCK // 2)
    hot_in[:, t, half_block] = own_hot[:, half_block]
    for c in loads[1:10]:
        c.wait()
    turn[...] = jnp.zeros_like(turn)
    for f in range(feats):
        turn[f * bag:(f + 1) * bag, :] = ids_ref[f].astype(F32)
    ids_cols[...] = turn[...].T
    spot = lax.broadcasted_iota(jnp.int32, (bag, batch), 0)
    for f in range(feats):
        live = spot < length_ref[f:f + 1, :]
        turn[f * bag:(f + 1) * bag, :] = jnp.where(live, weight_ref[f], 0.0)
    coef_cols[...] = turn[...].T

    def build_group(g):
        at = pl.ds(pl.multiple_of(g * group, group), group)
        ids = ids_cols[at, :]
        coef = coef_cols[at, :]
        lane = lax.broadcasted_iota(jnp.int32, (group, cache), 1).astype(F32)
        for f in range(feats):
            total = None
            for l in range(bag):
                j = f * bag + l
                term = jnp.where(ids[:, j:j + 1] == lane, coef[:, j:j + 1], 0.0)
                total = term if total is None else total + term
            high = total.astype(BF16)
            pick[f, at, :] = high
            pick_low[f, at, :] = (total - high.astype(F32)).astype(BF16)

    def build(first, last):
        @pl.loop(first, last)
        def _(g):
            build_group(g)

    build(0, EARLY)
    pl.semaphore_wait(barrier, n_table - 1 + n_rep - 1)

    id_copies = [
        remote(want_v.at[table_peer(k)[0]], ask.at[t], id_send.at[k], id_recv.at[k], table_peer(k))
        for k in range(1, n_table)
    ]
    hot_copies = [
        remote(own_hot.at[:, half_block], hot_in.at[:, t, half_block], hs_send.at[k],
               hs_recv.at[k], table_peer(k))
        for k in range(1, n_table)
    ]
    for c in id_copies + hot_copies:
        c.start()

    groups = batch // group
    first = groups * 3 // 4
    build(EARLY, first)
    for c in id_copies:
        c.wait()
    asked = [ask[p, w:w + 1, :] for p in range(n_table) for w in range(wants)]
    for i, rows in enumerate(pick_rows(asked, emb_ref)):
        serve[i // wants, i % wants] = rows
    cold_copies = [
        remote(serve.at[table_peer(k)[0]], cold_in.at[t], cs_send.at[k], cs_recv.at[k],
               table_peer(k))
        for k in range(1, n_table)
    ]
    for c in cold_copies:
        c.start()
    for c in hot_copies:
        c.wait()
    hot_mate = remote(
        hot_in.at[:, :, half_block], hot_in.at[:, :, half_block], m_send.at[0], m_recv.at[0], mate
    )
    hot_mate.start()
    cold_in[t] = serve[t]
    ag_ids[r] = ask[...]
    id_shares = [
        remote(ask, ag_ids.at[r], i_send.at[k], i_recv.at[k], rep_peer(k)) for k in range(1, n_rep)
    ]
    for c in id_shares:
        c.start()
    second = groups * 3 // 4
    build(first, second)

    bottom = jnp.zeros((batch, EMB), F32) + bb_ref[...]
    features = dense_ref.shape[0]
    turn[0:features, :] = dense_ref[...]
    turn[features:features + 1, :] = label_ref[...].astype(F32)
    dense = turn[...].T
    label = dense[:, features:features + 1]
    for j in range(features):
        bottom = bottom + dense[:, j:j + 1] * bw_ref[j:j + 1, :]
    lsum = jnp.zeros((batch, LANES), F32)

    def settle(lsum, j, value):
        cols = slice(j * EMB, (j + 1) * EMB)
        b = value.astype(BF16)
        base[0:batch, cols] = b
        x = b.astype(F32) * outw_ref[cols].reshape(1, -1)
        bow[:, cols] = x.astype(BF16)
        return lsum + x * (bias_ref[cols].reshape(1, -1) + 1.0)

    lsum = settle(lsum, 0, jnp.maximum(bottom, 0.0))
    cold = n_table * wants * BLOCK
    some = 2 if feats % 2 == 0 else 1

    def pool(f, cols, rows):
        at = slice(f, f + some)
        return jnp.dot(
            pick[at, :, cols].reshape(some * batch, -1), rows, preferred_element_type=F32
        ) + jnp.dot(
            pick_low[at, :, cols].reshape(some * batch, -1), rows, preferred_element_type=F32
        )

    def pool_hot(start, count, rows):
        at = pl.ds(start, count)
        many = max(2 * batch // count, 1)
        for f in range(0, feats, many):
            to = min(f + many, feats)
            m = (to - f) * count
            pooled = jnp.dot(
                pick[f:to, at, cold:].reshape(m, -1), rows, preferred_element_type=F32
            ) + jnp.dot(
                pick_low[f:to, at, cold:].reshape(m, -1), rows, preferred_element_type=F32
            )
            for i in range(to - f):
                part_sum[at, (f + i) * EMB:(f + i + 1) * EMB] = pooled[i * count:(i + 1) * count]

    def turn_weights(n):
        for i in range(width // EMB // CHUNKS):
            cols = pl.ds(pl.multiple_of(n * (width // CHUNKS) + i * EMB, EMB), EMB)
            down_t[cols, :] = down_ref[:, cols].T
            up_t[cols, :] = up_ref[:, cols].T

    for c in loads[10:]:
        c.wait()
    hot_mate.wait()
    steps = groups - second
    each = second // steps * group

    @pl.loop(0, steps)
    def _(j):
        rows = hot_in[...].reshape(cache - cold, EMB)
        pool_hot(pl.multiple_of(j * each, group), each, rows)
        turn_weights(j)
        build_group(second + j)

    done = steps * each
    pool_hot(done, batch - done, hot_in[...].reshape(cache - cold, EMB))
    for n in range(steps, CHUNKS):
        turn_weights(n)
    for c in cold_copies:
        c.wait()
    rows = cold_in[...].reshape(cold, EMB)
    wide = width // CHUNKS
    base_copies = []
    for f in range(0, feats, some):
        pooled = pool(f, slice(0, cold), rows)
        for i in range(some):
            before = part_sum[:, (f + i) * EMB:(f + i + 1) * EMB]
            lsum = settle(lsum, f + i + 1, pooled[i * batch:(i + 1) * batch] + before)
        n = len(base_copies)
        while n < CHUNKS and (f + some + 1) * EMB >= (n + 1) * wide:
            cols = slice(n * wide, (n + 1) * wide)
            base_copies.append(remote(
                base.at[0:batch, cols], base.at[batch:2 * batch, cols], b_send.at[n],
                b_recv.at[n], mate,
            ))
            base_copies[n].start()
            n += 1

    low = jnp.dot(base[0:batch], down_t[...], preferred_element_type=F32)
    high = jnp.dot(bow[...], up_t[...], preferred_element_type=F32)
    low_b = low.astype(BF16)
    prod = low_b.astype(F32) * high
    rank = prod.shape[1]
    for i in range(rank // LANES):
        lsum = lsum + prod[:, i * LANES:(i + 1) * LANES]
    logit = jnp.sum(lsum, axis=1, keepdims=True)
    lgrad = jax.nn.sigmoid(logit) - label
    g_low_f = high * lgrad
    g_low = g_low_f.astype(BF16)
    chips, two = acc.shape[0], acc.shape[1]
    own = two // 2
    turned = jnp.concatenate([low * lgrad, g_low_f], axis=1).T
    turned = turned.reshape(2, chips, 2, own, batch)
    is_first = core == 0
    mine = jnp.where(is_first, turned[:, :, 0], turned[:, :, 1])
    other = jnp.where(is_first, turned[:, :, 1], turned[:, :, 0])
    x_send[...] = other.reshape(rank, batch).astype(BF16)
    x_copy = remote(x_send, x_in, m_send.at[1], m_recv.at[1], mate)
    x_copy.start()
    x_own[...] = mine.reshape(rank, batch).astype(BF16)

    def bit_of(axis, bit):
        return lax.rem((t if axis == "table" else r) // (1 << bit), 2)

    def partner(axis, bit):
        shift = (1 - 2 * bit_of(axis, bit)) * (1 << bit)
        return (t + shift, r) if axis == "table" else (t, r + shift)

    parts = len(plan)
    step = width // parts
    lows = [0] * parts
    sizes = [chips] * parts
    copies = {}
    deep = len(stages[0])

    def launch(p, s):
        axis, bit = stages[p][s]
        at_bit = bit_of(axis, bit)
        half = sizes[p] // 2
        keep = lows[p] + at_bit * half
        give = lows[p] + (1 - at_bit) * half
        cols = slice(p * step, (p + 1) * step)
        i = p * deep + s
        sends[i][...] = acc[pl.ds(give, half), :, cols].astype(BF16)
        copies[p, s] = remote(sends[i], recvs[i], w_send.at[i], w_recv.at[i], partner(axis, bit))
        copies[p, s].start()
        lows[p], sizes[p] = keep, half

    def absorb(p, s):
        copies[p, s].wait()
        i = p * deep + s
        cols = slice(p * step, (p + 1) * step)
        at = pl.ds(lows[p], sizes[p])
        total = acc[at, :, cols] + recvs[i][...].astype(F32)
        if s + 1 < deep:
            acc[at, :, cols] = total
        else:
            up_out[:, cols] = total[0, 0:own]
            down_out[:, cols] = total[0, own:]

    def table_gradient(c):
        at = slice(c * wide, (c + 1) * wide)
        gate = jnp.dot(low_b, up_ref[:, at], preferred_element_type=F32)
        gate = gate + (bias_ref[at].reshape(1, -1) + 1.0)
        grad = (lgrad * outw_ref[at].reshape(1, -1)) * gate + jnp.dot(
            g_low, down_ref[:, at], preferred_element_type=F32
        )
        for i in range(wide // LANES):
            f = (c * wide) // LANES + i - 1
            if f >= 0:
                grad_t[:, f * batch:(f + 1) * batch] = (
                    grad[:, i * LANES:(i + 1) * LANES].T.astype(BF16)
                )

    for c in range(3 * CHUNKS // 3):
        table_gradient(c)
    for c in base_copies:
        c.wait()
    x_copy.wait()
    factors = jnp.concatenate([x_own[...], x_in[...]], axis=1)
    for c in range(CHUNKS):
        at = slice(c * wide, (c + 1) * wide)
        both = jnp.dot(factors, base[:, at], preferred_element_type=F32)
        up = both[0:rank // 2] * outw_ref[at].reshape(1, -1)
        down = both[rank // 2:]
        for i in range(parts // CHUNKS):
            p = c * (parts // CHUNKS) + i
            part, cols = slice(i * step, (i + 1) * step), slice(p * step, (p + 1) * step)
            for d in range(chips):
                rows_d = slice(d * own, (d + 1) * own)
                acc[plan[p][d], 0:own, cols] = up[rows_d, part]
                acc[plan[p][d], own:two, cols] = down[rows_d, part]
            launch(p, 0)

    for c in range(3 * CHUNKS // 3, CHUNKS):
        table_gradient(c)
    total = jnp.dot(
        grad_t[...], pick[...].reshape(feats * batch, cache), preferred_element_type=F32
    ).T
    tg_cold[...] = total[:cold].astype(BF16).reshape(tg_cold.shape)
    out_copies = []
    for k in range(1, n_table):
        to = table_peer(k)
        out_copies.append(
            remote(tg_cold.at[to[0]], ag_cold.at[r, t], c_send.at[k], c_recv.at[k], to)
        )
    for c in out_copies:
        c.start()
    ag_cold[r, t] = tg_cold[t]
    halves = total[cold:].reshape(slots, n_table, 2, BLOCK // 2, EMB)
    other = jnp.where(is_first, halves[:, :, 1], halves[:, :, 0])
    mine = jnp.where(is_first, halves[:, :, 0], halves[:, :, 1])
    folds = n_table.bit_length() - 1
    for o in range(n_table):
        at = sum(((o >> b) & 1) << (folds - 1 - b) for b in range(folds))
        for s in range(slots):
            hot_send[at, s] = other[s, o].astype(BF16)
            acc_hot[at, s] = mine[s, o]
    hot_pair = remote(hot_send, hot_recv, m_send.at[2], m_recv.at[2], mate)
    hot_pair.start()
    hot_at = [0, n_table]
    hot_copies = []

    def hot_launch():
        b = len(hot_copies)
        half = hot_at[1] // 2
        at_bit = bit_of("table", b)
        keep, give = hot_at[0] + at_bit * half, hot_at[0] + (1 - at_bit) * half
        span = pl.ds(n_table - 2 * half, half)
        fold_send[span] = acc_hot[pl.ds(give, half)].astype(BF16)
        hot_copies.append(remote(
            fold_send.at[span], fold_recv.at[span], f_send.at[b], f_recv.at[b],
            partner("table", b),
        ))
        hot_copies[b].start()
        hot_at[:] = [keep, half]

    def hot_absorb():
        hot_copies[-1].wait()
        at, half = pl.ds(hot_at[0], hot_at[1]), hot_at[1]
        span = slice(n_table - 2 * half, n_table - half)
        acc_hot[at] = acc_hot[at] + fold_recv[span].astype(F32)

    rep_bits = n_rep.bit_length() - 1
    hot_shares = []

    def hot_step(n):
        if n < folds:
            hot_absorb()
            if n + 1 < folds:
                hot_launch()
            else:
                hot_all[0] = acc_hot[hot_at[0]]
        elif n < folds + rep_bits - 1:
            hot_shares[-1].wait()
            k = n - folds
            hot_all[k + 1] = hot_all[k] + hot_there[k]
        k = n - folds + 1
        if 0 <= k < rep_bits:
            to = partner("replica", k + 1) if k + 1 < rep_bits else mate
            hot_shares.append(
                remote(hot_all.at[k], hot_there.at[k], g_send.at[k], g_recv.at[k], to)
            )
            hot_shares[k].start()

    hot_pair.wait()
    acc_hot[...] = acc_hot[...] + hot_recv[...].astype(F32)
    hot_launch()

    across = (t, lax.rem(r + n_rep // 2, n_rep))
    shares = []

    def share():
        for c in out_copies:
            c.wait()
        for n, to in enumerate((across, mate)):
            shares.append(remote(ag_cold.at[r], ag_cold.at[r], a_send.at[n], a_recv.at[n], to))
            shares[n].start()

    def forward():
        shares[0].wait()
        there = lax.rem(r + n_rep // 2, n_rep)
        shares.append(
            remote(ag_cold.at[there], ag_cold.at[there], a_send.at[2], a_recv.at[2], mate)
        )
        shares[2].start()

    mine_blocks = table_out.shape[0]
    first_block = r * mine_blocks

    def finish_cold():
        for c in id_shares:
            c.wait()
        shares[1].wait()
        shares[2].wait()
        total = [jnp.zeros((BLOCK, EMB), F32) for _ in range(mine_blocks)]
        for q in range(n_rep):
            for o in range(n_table):
                for w in range(wants):
                    ids = ag_ids[q, o, w:w + 1, :] - first_block
                    val = ag_cold[q, o, w].astype(F32)
                    for b in range(mine_blocks):
                        total[b] = total[b] + jnp.where(ids == b, val, 0.0)
        for b in range(mine_blocks):
            table_out[b] = total[b]

    def finish_hot():
        hot_shares[-1].wait()
        ours, theirs = hot_all[rep_bits - 1], hot_there[rep_bits - 1]
        for b in range(mine_blocks):
            total = table_out[b]
            for h in range(slots):
                ids = jnp.where(hot_rows[h] >= 0, hot_rows[h] - first_block, -1)
                val = jnp.concatenate([
                    jnp.where(is_first, ours[h], theirs[h]), jnp.where(is_first, theirs[h], ours[h])
                ], axis=0)
                total = total + jnp.where(ids == b, val, 0.0)
            table_out[b] = total

    hot_steps = list(range(folds + rep_bits - 1))
    for s in range(deep):
        for p in range(parts):
            absorb(p, s)
            if s + 1 < deep:
                launch(p, s + 1)
            if hot_steps and p == HOT_AFTER[min(s, len(HOT_AFTER) - 1)]:
                hot_step(hot_steps.pop(0))
            if (s, p) == SHARE:
                share()
            if (s, p) == FORWARD:
                forward()
            if (s, p) == FINISH:
                finish_cold()
    while hot_steps:
        hot_step(hot_steps.pop(0))
    finish_hot()


def whole(
    plan, stages, n_table, n_rep, want, hot_ids, count, emb, ids, weight, length, dense, labels,
    up, down, bias, outw, bw, bb,
):
    feats, bag, batch = ids.shape
    padded = -(-feats * bag // LANES) * LANES
    devices = n_table * n_rep
    rank, width = up.shape
    own = rank // devices
    two, chips = 2 * own, devices // 2
    wants, slots = want.shape[2], hot_ids.shape[1]
    cache = n_table * (wants + slots) * BLOCK
    step = width // PARTS
    mine = emb.shape[0] // BLOCK // n_rep
    shapes = []
    for part in stages:
        size = chips
        for _ in part:
            size //= 2
            shapes.append(pltpu.VMEM((size, two, step), BF16))
    dma = pltpu.SemaphoreType.DMA
    one, many = pl.BlockSpec(memory_space=pltpu.SMEM), pl.BlockSpec(memory_space=pltpu.HBM)
    return pl.pallas_call(
        functools.partial(whole_kernel, plan, stages, n_table, n_rep, len(shapes)),
        out_shape=[
            pltpu.VMEM((own, width), F32),
            pltpu.VMEM((own, width), F32),
            pltpu.VMEM((mine, BLOCK, EMB), F32),
        ],
        in_specs=[one] * 3 + [many] * 12,
        out_specs=vmem(3),
        scratch_shapes=[
            pltpu.VMEM(a.shape, a.dtype)
            for a in (emb, ids, weight, length, dense, labels, up, down, bias, outw, bw, bb)
        ] + [
            pltpu.VMEM((n_table, wants, LANES), jnp.int32),
            pltpu.VMEM((n_table, wants, LANES), jnp.int32),
            pltpu.VMEM((n_table, wants, BLOCK, EMB), BF16),
            pltpu.VMEM((slots, BLOCK, EMB), BF16),
            pltpu.VMEM((n_table, wants, BLOCK, EMB), BF16),
            pltpu.VMEM((slots, n_table, BLOCK, EMB), BF16),
            pltpu.VMEM((feats, batch, cache), BF16),
            pltpu.VMEM((feats, batch, cache), BF16),
            pltpu.VMEM((2 * batch, width), BF16),
            pltpu.VMEM((batch, width), F32),
            pltpu.VMEM((batch, width), BF16),
            pltpu.VMEM((EMB, feats * batch), BF16),
            pltpu.VMEM((batch, padded), F32),
            pltpu.VMEM((batch, padded), F32),
            pltpu.VMEM((padded, batch), F32),
            pltpu.VMEM((width, rank), BF16),
            pltpu.VMEM((width, rank), BF16),
            pltpu.VMEM((rank, batch), BF16),
            pltpu.VMEM((rank, batch), BF16),
            pltpu.VMEM((rank, batch), BF16),
            pltpu.VMEM((chips, two, width), F32),
            pltpu.VMEM((n_table, slots, BLOCK // 2, EMB), F32),
        ] + [pltpu.VMEM((n_table, slots, BLOCK // 2, EMB), BF16)] * 4 + [
            pltpu.VMEM((n_rep.bit_length() - 1, slots, BLOCK // 2, EMB), F32),
            pltpu.VMEM((n_rep.bit_length() - 1, slots, BLOCK // 2, EMB), F32),
            pltpu.VMEM((n_table, wants, BLOCK, EMB), BF16),
            pltpu.VMEM((n_rep, n_table, wants, BLOCK, EMB), BF16),
            pltpu.VMEM((n_rep, n_table, wants, LANES), jnp.int32),
        ] + shapes + shapes + [dma((12,))] + [dma((n_table,))] * 6 + [dma((CHUNKS,))] * 2
        + [dma((len(shapes),))] * 2 + [dma((n_table,))] * 2 + [dma((3,))] * 2
        + [dma((n_rep,))] * 2 + [dma((n_table,))] * 2 + [dma((n_rep,))] * 2 + [dma((3,))] * 2,
        compiler_params=pltpu.CompilerParams(
            collective_id=0, has_side_effects=True, vmem_limit_bytes=60 * 2**20
        ),
        name="whole",
    )(want, hot_ids, count, emb, ids, weight, length, dense, labels, up, down, bias, outw, bw, bb)


def finish_kernel(*refs):
    n = len(refs) // 2
    sem = refs[-1]
    copies = [
        pltpu.make_async_copy(refs[i], refs[n + i], sem.at[i]) for i in range(n)
    ]
    for c in copies:
        c.start()
    for c in copies:
        c.wait()


def finish(*arrays):
    many = [pl.BlockSpec(memory_space=pltpu.VMEM)] * len(arrays)
    outs = [pl.BlockSpec(memory_space=pltpu.HBM)] * len(arrays)
    return pl.pallas_call(
        finish_kernel,
        out_shape=[jax.ShapeDtypeStruct(a.shape, a.dtype) for a in arrays],
        in_specs=many,
        out_specs=outs,
        scratch_shapes=[pltpu.SemaphoreType.DMA((len(arrays),))],
        name="finish",
    )(*arrays)


def make_stages(n_table, n_rep, parts):
    rep = [("replica", b) for b in range(1, n_rep.bit_length() - 1)]
    tab = [("table", b) for b in range(n_table.bit_length() - 1)]
    bits = rep + tab
    tail = bits[:-1]
    turned = [tail[p % len(tail):] + tail[:p % len(tail)] for p in range(parts)]
    swapped = [p % 3 == 0 for p in range(parts)]
    return [
        part[:-1] + bits[-1:] + part[-1:] if swap else part + bits[-1:]
        for part, swap in zip(turned, swapped)
    ]


def places(stages, n_rep, chips):
    plan = []
    pairs = n_rep // 2
    for part in stages:
        row = []
        for d in range(chips):
            at = 0
            for axis, bit in part:
                number = d // pairs if axis == "table" else (d % pairs) * 2
                at = at * 2 + (number >> bit) % 2
            row.append(at)
        plan.append(row)
    return plan


def fast_local(
    emb_table, cross_up, cross_down, cross_bias, out_weight, bottom_weight, bottom_bias,
    dense_in, labels, lookup_ids, bag_weight, bag_length, want_blocks, hot_blocks, hot_count,
):
    owners, reps = lax.axis_size("table"), lax.axis_size("replica")
    stages = make_stages(owners, reps, PARTS)
    plan = places(stages, reps, owners * reps // 2)
    up, down, table = whole(
        plan, stages, owners, reps, want_blocks.transpose(0, 1, 3, 2), hot_blocks, hot_count, emb_table,
        lookup_ids.transpose(1, 2, 0), bag_weight.transpose(1, 2, 0), bag_length.T,
        dense_in.T, labels[None], cross_up, cross_down, cross_bias, out_weight,
        bottom_weight, bottom_bias[None],
    )
    up, down, table = [pltpu.with_memory_space_constraint(a, pltpu.VMEM) for a in (up, down, table)]
    u, d, t = finish(up, down, table)
    return u, d, t.reshape(-1, EMB)


def local_step(
    cached_rows,
    dense_dev,
    labels_dev,
    ids_dev,
    weight_dev,
    length_dev,
    cross_up,
    cross_down,
    cross_bias,
    out_weight,
    bottom_weight,
    bottom_bias,
):
    batch = ids_dev.shape[0]
    width = cached_rows.shape[1]
    gathered = cached_rows[ids_dev].astype(jnp.float32)
    slots = jnp.arange(ids_dev.shape[2], dtype=jnp.int32)
    bag_coef = jnp.where(
        slots[None, None, :] < length_dev[:, :, None], weight_dev, jnp.zeros((), jnp.float32)
    )
    pooled = jnp.sum(bag_coef[..., None] * gathered, axis=2)
    bottom = jax.nn.relu(
        jnp.dot(dense_dev, bottom_weight, precision=lax.Precision.HIGHEST) + bottom_bias
    )
    cross_base = jnp.concatenate([bottom, pooled.reshape(batch, -1)], 1).astype(jnp.bfloat16)
    low_rank = lax.dot_general(
        cross_base, cross_down, (((1,), (1,)), ((), ())), preferred_element_type=jnp.float32
    ).astype(jnp.bfloat16)
    cross_gate = jnp.dot(low_rank, cross_up, preferred_element_type=jnp.float32) + cross_bias
    base_wide = cross_base.astype(jnp.float32)
    crossed = base_wide * cross_gate + base_wide
    logits = jnp.dot(crossed, out_weight, precision=lax.Precision.HIGHEST)
    logit_grad = jax.nn.sigmoid(logits) - labels_dev.astype(jnp.float32)
    grad_crossed = logit_grad[:, None] * out_weight[None, :]
    g_cross = (grad_crossed * base_wide).astype(jnp.bfloat16)
    g_low = lax.dot_general(
        g_cross, cross_up, (((1,), (1,)), ((), ())), preferred_element_type=jnp.float32
    ).astype(jnp.bfloat16)
    up_part = lax.dot_general(
        low_rank, g_cross, (((0,), (0,)), ((), ())), preferred_element_type=jnp.float32
    )
    down_part = lax.dot_general(
        g_low, cross_base, (((0,), (0,)), ((), ())), preferred_element_type=jnp.float32
    )
    grad_base = grad_crossed * (cross_gate + 1.0) + jnp.dot(
        g_low, cross_down, preferred_element_type=jnp.float32
    )
    grad_pooled = grad_base[:, width:].reshape(batch, -1, width)
    contrib = bag_coef[..., None] * grad_pooled[:, :, None, :]
    cache_grad = (
        jnp.zeros(cached_rows.shape, jnp.float32)
        .at[ids_dev.reshape(-1)]
        .add(contrib.reshape(-1, width))
    )
    return (up_part, down_part, cache_grad)


def plain_local(
    emb_table,
    cross_up,
    cross_down,
    cross_bias,
    out_weight,
    bottom_weight,
    bottom_bias,
    dense_in,
    labels,
    lookup_ids,
    bag_weight,
    bag_length,
    want_blocks,
    hot_blocks,
    hot_count,
):
    owners = lax.axis_size("table")
    blocks = emb_table.reshape(-1, BLOCK, EMB)
    block_total = blocks.shape[0]
    wanted = want_blocks.reshape(owners, want_blocks.shape[3])
    asked_for = lax.all_to_all(wanted, "table", split_axis=0, concat_axis=0, tiled=True)
    flat = emb_table.reshape(block_total, -1)
    numbers = jnp.arange(block_total, dtype=jnp.int32)

    def take(ids):
        pick = (ids.reshape(-1)[:, None] == numbers[None, :]).astype(jnp.bfloat16)
        rows = jnp.dot(pick, flat, preferred_element_type=jnp.float32).astype(jnp.bfloat16)
        return rows.reshape(ids.shape + (BLOCK, EMB))

    served = take(asked_for)
    cold_rows = lax.all_to_all(served, "table", split_axis=0, concat_axis=0, tiled=True)
    slot_count = hot_blocks.shape[1]
    alive = jnp.arange(slot_count, dtype=jnp.int32) < hot_count[0]
    own_hot = jnp.where(alive[:, None, None], take(hot_blocks[0]), jnp.zeros((), jnp.bfloat16))
    hot_rows = lax.all_gather(own_hot[:, None], "table", axis=1, tiled=True)
    cold_count = cold_rows.shape[0] * cold_rows.shape[1] * BLOCK
    cached_rows = jnp.concatenate([cold_rows.reshape(-1, EMB), hot_rows.reshape(-1, EMB)], 0)
    up_part, down_part, cache_grad = local_step(
        cached_rows,
        dense_in,
        labels,
        lookup_ids,
        bag_weight,
        bag_length,
        cross_up,
        cross_down,
        cross_bias,
        out_weight,
        bottom_weight,
        bottom_bias,
    )
    cold_grad = cache_grad[:cold_count].reshape(cold_rows.shape).astype(jnp.bfloat16)
    returned = lax.all_to_all(cold_grad, "table", split_axis=0, concat_axis=0, tiled=True)
    hot_grad = cache_grad[cold_count:].reshape(hot_rows.shape)
    hot_sums = lax.psum_scatter(hot_grad, "table", scatter_dimension=1, tiled=True)[:, 0]
    block_ids = jnp.arange(block_total, dtype=jnp.int32)
    cold_pick = (asked_for.reshape(-1)[:, None] == block_ids[None, :]).astype(jnp.bfloat16)
    hot_pick = ((hot_blocks[0][:, None] == block_ids[None, :]) & alive[:, None]).astype(jnp.float32)
    block_grad = lax.dot_general(
        cold_pick,
        returned.reshape(cold_pick.shape[0], -1),
        (((0,), (0,)), ((), ())),
        preferred_element_type=jnp.float32,
    )
    block_grad = block_grad + lax.dot_general(
        hot_pick,
        hot_sums.reshape(slot_count, -1),
        (((0,), (0,)), ((), ())),
        precision=lax.Precision.HIGHEST,
    )
    table_grad = lax.psum_scatter(
        block_grad.reshape(-1, EMB), "replica", scatter_dimension=0, tiled=True
    )
    up_grad, down_grad = (
        lax.psum_scatter(up_part, ("table", "replica"), scatter_dimension=0, tiled=True),
        lax.psum_scatter(down_part, ("table", "replica"), scatter_dimension=0, tiled=True),
    )
    return (up_grad, down_grad, table_grad)


def choose(mesh, *args):
    devices = mesh.shape["table"] * mesh.shape["replica"]
    powers = all(n > 1 and n & (n - 1) == 0 for n in mesh.shape.values())
    rank, width = args[1].shape
    ids, want, hot = args[9], args[12], args[13]
    cache = mesh.shape["table"] * (want.shape[3] + hot.shape[1]) * BLOCK
    picked = 2 * ids.shape[0] * ids.shape[1] * cache
    whole_tiles = rank % (devices * SUBLANES) == 0 and width % (PARTS * LANES) == 0
    if powers and whole_tiles and ids.shape[0] == LANES and picked < 2**23:
        return fast_local(*args)
    return plain_local(*args)


def solution(mesh):
    local = functools.partial(choose, mesh)
    placed = (
        P("table", None),
        P(),
        P(),
        P(),
        P(),
        P(),
        P(),
        P(("table", "replica"), None),
        P(("table", "replica")),
        P(("table", "replica"), None, None),
        P(("table", "replica"), None, None),
        P(("table", "replica"), None),
        P("table", "replica", None, None),
        P("table", None),
        P("table"),
    )
    return jax.shard_map(
        local,
        mesh=mesh,
        in_specs=placed,
        out_specs=(
            P(("table", "replica"), None),
            P(("table", "replica"), None),
            P(("table", "replica"), None),
        ),
        check_vma=False,
    )
```

```python
import functools

import jax
import jax.numpy as jnp
from jax import lax
from jax.experimental import pallas as pl
from jax.experimental.pallas import tpu as pltpu
from jax.sharding import PartitionSpec as P

EMB = 128
BLOCK = 32
LANES = 128
SUBLANES = 8
MESH = pl.DeviceIdType.MESH
CHUNKS = 3
PARTS = 9
EARLY = 1
SHARE, FORWARD, FINISH = (1, 8), (2, 8), (3, 6)
HOT_AFTER = (5, 2, 0, 0)
F32 = jnp.float32
BF16 = jnp.bfloat16


def vmem(n):
    return [pl.BlockSpec(memory_space=pltpu.VMEM)] * n


def pick_rows(ids, emb_ref):
    found = [jnp.zeros((BLOCK, EMB), F32) for _ in ids]
    for b in range(emb_ref.shape[0] // BLOCK):
        block = emb_ref[b * BLOCK:(b + 1) * BLOCK, :].astype(F32)
        found = [jnp.where(i == b, block, f) for i, f in zip(ids, found)]
    return [f.astype(BF16) for f in found]


def whole_kernel(
    plan, stages, n_table, n_rep, buffers,
    want_ref, hot_ids_ref, count_ref, emb_hbm, ids_hbm, weight_hbm, length_hbm, dense_hbm,
    label_hbm, up_hbm, down_hbm, bias_hbm, outw_hbm, bw_hbm, bb_hbm,
    up_out, down_out, table_out,
    emb_ref, ids_ref, weight_ref, length_ref, dense_ref, label_ref, up_ref, down_ref,
    bias_ref, outw_ref, bw_ref, bb_ref, want_v, ask, serve, own_hot, cold_in, hot_in,
    pick, pick_low, base, part_sum, bow, grad_t, ids_cols, coef_cols, turn,
    down_t, up_t, x_own, x_send, x_in, acc, acc_hot, hot_send, hot_recv, fold_send, fold_recv, hot_all,
    hot_there, tg_cold, ag_cold, ag_ids,
    *rest,
):
    sends = rest[:buffers]
    recvs = rest[buffers:2 * buffers]
    (load_sem, id_send, id_recv, hs_send, hs_recv, cs_send, cs_recv, b_send, b_recv,
     w_send, w_recv, c_send, c_recv, a_send, a_recv, i_send, i_recv, f_send, f_recv,
     g_send, g_recv, m_send, m_recv) = rest[2 * buffers:]
    t = lax.axis_index("table")
    r = lax.axis_index("replica")
    wants = serve.shape[1]
    slots = own_hot.shape[0]
    feats, batch, cache = pick.shape
    bag = ids_ref.shape[1]
    width = base.shape[1]
    group = 16
    core = lax.rem(r, 2)
    mate = (t, r + 1 - 2 * core)

    def table_peer(k):
        return (lax.rem(t + k, n_table), r)

    def rep_peer(k):
        return (t, lax.rem(r + k, n_rep))

    def remote(src, dst, send, recv, device):
        return pltpu.make_async_remote_copy(
            src_ref=src, dst_ref=dst, send_sem=send, recv_sem=recv,
            device_id=device, device_id_type=MESH,
        )

    barrier = pltpu.get_barrier_semaphore()
    for k in range(1, n_table):
        pl.semaphore_signal(barrier, inc=1, device_id=table_peer(k), device_id_type=MESH)
    for k in range(1, n_rep):
        pl.semaphore_signal(barrier, inc=1, device_id=rep_peer(k), device_id_type=MESH)
    loads = [
        pltpu.make_async_copy(src, dst, load_sem.at[i])
        for i, (src, dst) in enumerate((
            (emb_hbm, emb_ref), (ids_hbm, ids_ref), (weight_hbm, weight_ref),
            (length_hbm, length_ref), (dense_hbm, dense_ref), (label_hbm, label_ref),
            (bw_hbm, bw_ref), (bb_hbm, bb_ref), (bias_hbm, bias_ref), (outw_hbm, outw_ref),
            (down_hbm, down_ref), (up_hbm, up_ref),
        ))
    ]
    for c in loads:
        c.start()
    for p in range(n_table):
        for w in range(wants):
            want_v[p, w:w + 1] = jnp.full((1, LANES), want_ref[0, 0, w, p], jnp.int32)
    ask[t] = want_v[t]
    hot_rows = []
    for s in range(slots):
        block = jnp.where(s < count_ref[0], hot_ids_ref[0, s], -1)
        hot_rows.append(jnp.full((1, LANES), block, jnp.int32))

    loads[0].wait()
    for s, rows in enumerate(pick_rows(hot_rows, emb_ref)):
        own_hot[s] = rows
    half_block = pl.ds(pl.multiple_of(core * (BLOCK // 2), BLOCK // 2), BLOCK // 2)
    hot_in[:, t, half_block] = own_hot[:, half_block]
    for c in loads[1:10]:
        c.wait()
    turn[...] = jnp.zeros_like(turn)
    for f in range(feats):
        turn[f * bag:(f + 1) * bag, :] = ids_ref[f].astype(F32)
    ids_cols[...] = turn[...].T
    spot = lax.broadcasted_iota(jnp.int32, (bag, batch), 0)
    for f in range(feats):
        live = spot < length_ref[f:f + 1, :]
        turn[f * bag:(f + 1) * bag, :] = jnp.where(live, weight_ref[f], 0.0)
    coef_cols[...] = turn[...].T

    def build_group(g):
        at = pl.ds(pl.multiple_of(g * group, group), group)
        ids = ids_cols[at, :]
        coef = coef_cols[at, :]
        lane = lax.broadcasted_iota(jnp.int32, (group, cache), 1).astype(F32)
        for f in range(feats):
            total = None
            for l in range(bag):
                j = f * bag + l
                term = jnp.where(ids[:, j:j + 1] == lane, coef[:, j:j + 1], 0.0)
                total = term if total is None else total + term
            high = total.astype(BF16)
            pick[f, at, :] = high
            pick_low[f, at, :] = (total - high.astype(F32)).astype(BF16)

    def build(first, last):
        @pl.loop(first, last)
        def _(g):
            build_group(g)

    build(0, EARLY)
    pl.semaphore_wait(barrier, n_table - 1 + n_rep - 1)

    id_copies = [
        remote(want_v.at[table_peer(k)[0]], ask.at[t], id_send.at[k], id_recv.at[k], table_peer(k))
        for k in range(1, n_table)
    ]
    hot_copies = [
        remote(own_hot.at[:, half_block], hot_in.at[:, t, half_block], hs_send.at[k],
               hs_recv.at[k], table_peer(k))
        for k in range(1, n_table)
    ]
    for c in id_copies + hot_copies:
        c.start()

    groups = batch // group
    first = groups * 3 // 4
    build(EARLY, first)
    for c in id_copies:
        c.wait()
    asked = [ask[p, w:w + 1, :] for p in range(n_table) for w in range(wants)]
    for i, rows in enumerate(pick_rows(asked, emb_ref)):
        serve[i // wants, i % wants] = rows
    cold_copies = [
        remote(serve.at[table_peer(k)[0]], cold_in.at[t], cs_send.at[k], cs_recv.at[k],
               table_peer(k))
        for k in range(1, n_table)
    ]
    for c in cold_copies:
        c.start()
    for c in hot_copies:
        c.wait()
    hot_mate = remote(
        hot_in.at[:, :, half_block], hot_in.at[:, :, half_block], m_send.at[0], m_recv.at[0], mate
    )
    hot_mate.start()
    cold_in[t] = serve[t]
    ag_ids[r] = ask[...]
    id_shares = [
        remote(ask, ag_ids.at[r], i_send.at[k], i_recv.at[k], rep_peer(k)) for k in range(1, n_rep)
    ]
    for c in id_shares:
        c.start()
    second = groups * 3 // 4
    build(first, second)

    bottom = jnp.zeros((batch, EMB), F32) + bb_ref[...]
    features = dense_ref.shape[0]
    turn[0:features, :] = dense_ref[...]
    turn[features:features + 1, :] = label_ref[...].astype(F32)
    dense = turn[...].T
    label = dense[:, features:features + 1]
    for j in range(features):
        bottom = bottom + dense[:, j:j + 1] * bw_ref[j:j + 1, :]
    lsum = jnp.zeros((batch, LANES), F32)

    def settle(lsum, j, value):
        cols = slice(j * EMB, (j + 1) * EMB)
        b = value.astype(BF16)
        base[0:batch, cols] = b
        x = b.astype(F32) * outw_ref[cols].reshape(1, -1)
        bow[:, cols] = x.astype(BF16)
        return lsum + x * (bias_ref[cols].reshape(1, -1) + 1.0)

    lsum = settle(lsum, 0, jnp.maximum(bottom, 0.0))
    cold = n_table * wants * BLOCK
    some = 2 if feats % 2 == 0 else 1

    def pool(f, cols, rows):
        at = slice(f, f + some)
        return jnp.dot(
            pick[at, :, cols].reshape(some * batch, -1), rows, preferred_element_type=F32
        ) + jnp.dot(
            pick_low[at, :, cols].reshape(some * batch, -1), rows, preferred_element_type=F32
        )

    def pool_hot(start, count, rows):
        at = pl.ds(start, count)
        many = max(2 * batch // count, 1)
        for f in range(0, feats, many):
            to = min(f + many, feats)
            m = (to - f) * count
            pooled = jnp.dot(
                pick[f:to, at, cold:].reshape(m, -1), rows, preferred_element_type=F32
            ) + jnp.dot(
                pick_low[f:to, at, cold:].reshape(m, -1), rows, preferred_element_type=F32
            )
            for i in range(to - f):
                part_sum[at, (f + i) * EMB:(f + i + 1) * EMB] = pooled[i * count:(i + 1) * count]

    def turn_weights(n):
        for i in range(width // EMB // CHUNKS):
            cols = pl.ds(pl.multiple_of(n * (width // CHUNKS) + i * EMB, EMB), EMB)
            down_t[cols, :] = down_ref[:, cols].T
            up_t[cols, :] = up_ref[:, cols].T

    for c in loads[10:]:
        c.wait()
    hot_mate.wait()
    steps = groups - second
    each = second // steps * group

    @pl.loop(0, steps)
    def _(j):
        rows = hot_in[...].reshape(cache - cold, EMB)
        pool_hot(pl.multiple_of(j * each, group), each, rows)
        turn_weights(j)
        build_group(second + j)

    done = steps * each
    pool_hot(done, batch - done, hot_in[...].reshape(cache - cold, EMB))
    for n in range(steps, CHUNKS):
        turn_weights(n)
    for c in cold_copies:
        c.wait()
    rows = cold_in[...].reshape(cold, EMB)
    wide = width // CHUNKS
    base_copies = []
    for f in range(0, feats, some):
        pooled = pool(f, slice(0, cold), rows)
        for i in range(some):
            before = part_sum[:, (f + i) * EMB:(f + i + 1) * EMB]
            lsum = settle(lsum, f + i + 1, pooled[i * batch:(i + 1) * batch] + before)
        n = len(base_copies)
        while n < CHUNKS and (f + some + 1) * EMB >= (n + 1) * wide:
            cols = slice(n * wide, (n + 1) * wide)
            base_copies.append(remote(
                base.at[0:batch, cols], base.at[batch:2 * batch, cols], b_send.at[n],
                b_recv.at[n], mate,
            ))
            base_copies[n].start()
            n += 1

    low = jnp.dot(base[0:batch], down_t[...], preferred_element_type=F32)
    high = jnp.dot(bow[...], up_t[...], preferred_element_type=F32)
    low_b = low.astype(BF16)
    prod = low_b.astype(F32) * high
    rank = prod.shape[1]
    for i in range(rank // LANES):
        lsum = lsum + prod[:, i * LANES:(i + 1) * LANES]
    logit = jnp.sum(lsum, axis=1, keepdims=True)
    lgrad = jax.nn.sigmoid(logit) - label
    g_low_f = high * lgrad
    g_low = g_low_f.astype(BF16)
    chips, two = acc.shape[0], acc.shape[1]
    own = two // 2
    turned = jnp.concatenate([low * lgrad, g_low_f], axis=1).T
    turned = turned.reshape(2, chips, 2, own, batch)
    is_first = core == 0
    mine = jnp.where(is_first, turned[:, :, 0], turned[:, :, 1])
    other = jnp.where(is_first, turned[:, :, 1], turned[:, :, 0])
    x_send[...] = other.reshape(rank, batch).astype(BF16)
    x_copy = remote(x_send, x_in, m_send.at[1], m_recv.at[1], mate)
    x_copy.start()
    x_own[...] = mine.reshape(rank, batch).astype(BF16)

    def bit_of(axis, bit):
        return lax.rem((t if axis == "table" else r) // (1 << bit), 2)

    def partner(axis, bit):
        shift = (1 - 2 * bit_of(axis, bit)) * (1 << bit)
        return (t + shift, r) if axis == "table" else (t, r + shift)

    parts = len(plan)
    step = width // parts
    lows = [0] * parts
    sizes = [chips] * parts
    copies = {}
    deep = len(stages[0])

    def launch(p, s):
        axis, bit = stages[p][s]
        at_bit = bit_of(axis, bit)
        half = sizes[p] // 2
        keep = lows[p] + at_bit * half
        give = lows[p] + (1 - at_bit) * half
        cols = slice(p * step, (p + 1) * step)
        i = p * deep + s
        sends[i][...] = acc[pl.ds(give, half), :, cols].astype(BF16)
        copies[p, s] = remote(sends[i], recvs[i], w_send.at[i], w_recv.at[i], partner(axis, bit))
        copies[p, s].start()
        lows[p], sizes[p] = keep, half

    def absorb(p, s):
        copies[p, s].wait()
        i = p * deep + s
        cols = slice(p * step, (p + 1) * step)
        at = pl.ds(lows[p], sizes[p])
        total = acc[at, :, cols] + recvs[i][...].astype(F32)
        if s + 1 < deep:
            acc[at, :, cols] = total
        else:
            up_out[:, cols] = total[0, 0:own]
            down_out[:, cols] = total[0, own:]

    for c in base_copies:
        c.wait()
    x_copy.wait()
    factors = jnp.concatenate([x_own[...], x_in[...]], axis=1)
    for c in range(CHUNKS):
        at = slice(c * wide, (c + 1) * wide)
        both = jnp.dot(factors, base[:, at], preferred_element_type=F32)
        up = both[0:rank // 2] * outw_ref[at].reshape(1, -1)
        down = both[rank // 2:]
        for i in range(parts // CHUNKS):
            p = c * (parts // CHUNKS) + i
            part, cols = slice(i * step, (i + 1) * step), slice(p * step, (p + 1) * step)
            for d in range(chips):
                rows_d = slice(d * own, (d + 1) * own)
                acc[plan[p][d], 0:own, cols] = up[rows_d, part]
                acc[plan[p][d], own:two, cols] = down[rows_d, part]
            launch(p, 0)

    for c in range(CHUNKS):
        at = slice(c * wide, (c + 1) * wide)
        gate = jnp.dot(low_b, up_ref[:, at], preferred_element_type=F32)
        gate = gate + (bias_ref[at].reshape(1, -1) + 1.0)
        grad = (lgrad * outw_ref[at].reshape(1, -1)) * gate + jnp.dot(
            g_low, down_ref[:, at], preferred_element_type=F32
        )
        for i in range(wide // LANES):
            f = (c * wide) // LANES + i - 1
            if f >= 0:
                grad_t[:, f * batch:(f + 1) * batch] = (
                    grad[:, i * LANES:(i + 1) * LANES].T.astype(BF16)
                )
    total = jnp.dot(
        grad_t[...], pick[...].reshape(feats * batch, cache), preferred_element_type=F32
    ).T
    tg_cold[...] = total[:cold].astype(BF16).reshape(tg_cold.shape)
    out_copies = []
    for k in range(1, n_table):
        to = table_peer(k)
        out_copies.append(
            remote(tg_cold.at[to[0]], ag_cold.at[r, t], c_send.at[k], c_recv.at[k], to)
        )
    ag_cold[r, t] = tg_cold[t]
    halves = total[cold:].reshape(slots, n_table, 2, BLOCK // 2, EMB)
    other = jnp.where(is_first, halves[:, :, 1], halves[:, :, 0])
    mine = jnp.where(is_first, halves[:, :, 0], halves[:, :, 1])
    folds = n_table.bit_length() - 1
    for o in range(n_table):
        at = sum(((o >> b) & 1) << (folds - 1 - b) for b in range(folds))
        for s in range(slots):
            hot_send[at, s] = other[s, o].astype(BF16)
            acc_hot[at, s] = mine[s, o]
    hot_pair = remote(hot_send, hot_recv, m_send.at[2], m_recv.at[2], mate)
    hot_pair.start()
    hot_at = [0, n_table]
    hot_copies = []

    def hot_launch():
        b = len(hot_copies)
        half = hot_at[1] // 2
        at_bit = bit_of("table", b)
        keep, give = hot_at[0] + at_bit * half, hot_at[0] + (1 - at_bit) * half
        span = pl.ds(n_table - 2 * half, half)
        fold_send[span] = acc_hot[pl.ds(give, half)].astype(BF16)
        hot_copies.append(remote(
            fold_send.at[span], fold_recv.at[span], f_send.at[b], f_recv.at[b],
            partner("table", b),
        ))
        hot_copies[b].start()
        hot_at[:] = [keep, half]

    def hot_absorb():
        hot_copies[-1].wait()
        at, half = pl.ds(hot_at[0], hot_at[1]), hot_at[1]
        span = slice(n_table - 2 * half, n_table - half)
        acc_hot[at] = acc_hot[at] + fold_recv[span].astype(F32)

    rep_bits = n_rep.bit_length() - 1
    hot_shares = []

    def hot_step(n):
        if n < folds:
            hot_absorb()
            if n + 1 < folds:
                hot_launch()
            else:
                hot_all[0] = acc_hot[hot_at[0]]
        elif n < folds + rep_bits - 1:
            hot_shares[-1].wait()
            k = n - folds
            hot_all[k + 1] = hot_all[k] + hot_there[k]
        k = n - folds + 1
        if 0 <= k < rep_bits:
            to = partner("replica", k + 1) if k + 1 < rep_bits else mate
            hot_shares.append(
                remote(hot_all.at[k], hot_there.at[k], g_send.at[k], g_recv.at[k], to)
            )
            hot_shares[k].start()

    for c in out_copies:
        c.start()
    hot_pair.wait()
    acc_hot[...] = acc_hot[...] + hot_recv[...].astype(F32)
    hot_launch()

    across = (t, lax.rem(r + n_rep // 2, n_rep))
    shares = []

    def share():
        for c in out_copies:
            c.wait()
        for n, to in enumerate((across, mate)):
            shares.append(remote(ag_cold.at[r], ag_cold.at[r], a_send.at[n], a_recv.at[n], to))
            shares[n].start()

    def forward():
        shares[0].wait()
        there = lax.rem(r + n_rep // 2, n_rep)
        shares.append(
            remote(ag_cold.at[there], ag_cold.at[there], a_send.at[2], a_recv.at[2], mate)
        )
        shares[2].start()

    mine_blocks = table_out.shape[0]
    first_block = r * mine_blocks

    def finish_cold():
        for c in id_shares:
            c.wait()
        shares[1].wait()
        shares[2].wait()
        total = [jnp.zeros((BLOCK, EMB), F32) for _ in range(mine_blocks)]
        for q in range(n_rep):
            for o in range(n_table):
                for w in range(wants):
                    ids = ag_ids[q, o, w:w + 1, :] - first_block
                    val = ag_cold[q, o, w].astype(F32)
                    for b in range(mine_blocks):
                        total[b] = total[b] + jnp.where(ids == b, val, 0.0)
        for b in range(mine_blocks):
            table_out[b] = total[b]

    def finish_hot():
        hot_shares[-1].wait()
        ours, theirs = hot_all[rep_bits - 1], hot_there[rep_bits - 1]
        for b in range(mine_blocks):
            total = table_out[b]
            for h in range(slots):
                ids = jnp.where(hot_rows[h] >= 0, hot_rows[h] - first_block, -1)
                val = jnp.concatenate([
                    jnp.where(is_first, ours[h], theirs[h]), jnp.where(is_first, theirs[h], ours[h])
                ], axis=0)
                total = total + jnp.where(ids == b, val, 0.0)
            table_out[b] = total

    hot_steps = list(range(folds + rep_bits - 1))
    for s in range(deep):
        for p in range(parts):
            absorb(p, s)
            if s + 1 < deep:
                launch(p, s + 1)
            if hot_steps and p == HOT_AFTER[min(s, len(HOT_AFTER) - 1)]:
                hot_step(hot_steps.pop(0))
            if (s, p) == SHARE:
                share()
            if (s, p) == FORWARD:
                forward()
            if (s, p) == FINISH:
                finish_cold()
    while hot_steps:
        hot_step(hot_steps.pop(0))
    finish_hot()


def whole(
    plan, stages, n_table, n_rep, want, hot_ids, count, emb, ids, weight, length, dense, labels,
    up, down, bias, outw, bw, bb,
):
    feats, bag, batch = ids.shape
    padded = -(-feats * bag // LANES) * LANES
    devices = n_table * n_rep
    rank, width = up.shape
    own = rank // devices
    two, chips = 2 * own, devices // 2
    wants, slots = want.shape[2], hot_ids.shape[1]
    cache = n_table * (wants + slots) * BLOCK
    step = width // PARTS
    mine = emb.shape[0] // BLOCK // n_rep
    shapes = []
    for part in stages:
        size = chips
        for _ in part:
            size //= 2
            shapes.append(pltpu.VMEM((size, two, step), BF16))
    dma = pltpu.SemaphoreType.DMA
    one, many = pl.BlockSpec(memory_space=pltpu.SMEM), pl.BlockSpec(memory_space=pltpu.HBM)
    return pl.pallas_call(
        functools.partial(whole_kernel, plan, stages, n_table, n_rep, len(shapes)),
        out_shape=[
            pltpu.VMEM((own, width), F32),
            pltpu.VMEM((own, width), F32),
            pltpu.VMEM((mine, BLOCK, EMB), F32),
        ],
        in_specs=[one] * 3 + [many] * 12,
        out_specs=vmem(3),
        scratch_shapes=[
            pltpu.VMEM(a.shape, a.dtype)
            for a in (emb, ids, weight, length, dense, labels, up, down, bias, outw, bw, bb)
        ] + [
            pltpu.VMEM((n_table, wants, LANES), jnp.int32),
            pltpu.VMEM((n_table, wants, LANES), jnp.int32),
            pltpu.VMEM((n_table, wants, BLOCK, EMB), BF16),
            pltpu.VMEM((slots, BLOCK, EMB), BF16),
            pltpu.VMEM((n_table, wants, BLOCK, EMB), BF16),
            pltpu.VMEM((slots, n_table, BLOCK, EMB), BF16),
            pltpu.VMEM((feats, batch, cache), BF16),
            pltpu.VMEM((feats, batch, cache), BF16),
            pltpu.VMEM((2 * batch, width), BF16),
            pltpu.VMEM((batch, width), F32),
            pltpu.VMEM((batch, width), BF16),
            pltpu.VMEM((EMB, feats * batch), BF16),
            pltpu.VMEM((batch, padded), F32),
            pltpu.VMEM((batch, padded), F32),
            pltpu.VMEM((padded, batch), F32),
            pltpu.VMEM((width, rank), BF16),
            pltpu.VMEM((width, rank), BF16),
            pltpu.VMEM((rank, batch), BF16),
            pltpu.VMEM((rank, batch), BF16),
            pltpu.VMEM((rank, batch), BF16),
            pltpu.VMEM((chips, two, width), F32),
            pltpu.VMEM((n_table, slots, BLOCK // 2, EMB), F32),
        ] + [pltpu.VMEM((n_table, slots, BLOCK // 2, EMB), BF16)] * 4 + [
            pltpu.VMEM((n_rep.bit_length() - 1, slots, BLOCK // 2, EMB), F32),
            pltpu.VMEM((n_rep.bit_length() - 1, slots, BLOCK // 2, EMB), F32),
            pltpu.VMEM((n_table, wants, BLOCK, EMB), BF16),
            pltpu.VMEM((n_rep, n_table, wants, BLOCK, EMB), BF16),
            pltpu.VMEM((n_rep, n_table, wants, LANES), jnp.int32),
        ] + shapes + shapes + [dma((12,))] + [dma((n_table,))] * 6 + [dma((CHUNKS,))] * 2
        + [dma((len(shapes),))] * 2 + [dma((n_table,))] * 2 + [dma((3,))] * 2
        + [dma((n_rep,))] * 2 + [dma((n_table,))] * 2 + [dma((n_rep,))] * 2 + [dma((3,))] * 2,
        compiler_params=pltpu.CompilerParams(
            collective_id=0, has_side_effects=True, vmem_limit_bytes=60 * 2**20
        ),
        name="whole",
    )(want, hot_ids, count, emb, ids, weight, length, dense, labels, up, down, bias, outw, bw, bb)


def finish_kernel(*refs):
    n = len(refs) // 2
    sem = refs[-1]
    copies = [
        pltpu.make_async_copy(refs[i], refs[n + i], sem.at[i]) for i in range(n)
    ]
    for c in copies:
        c.start()
    for c in copies:
        c.wait()


def finish(*arrays):
    many = [pl.BlockSpec(memory_space=pltpu.VMEM)] * len(arrays)
    outs = [pl.BlockSpec(memory_space=pltpu.HBM)] * len(arrays)
    return pl.pallas_call(
        finish_kernel,
        out_shape=[jax.ShapeDtypeStruct(a.shape, a.dtype) for a in arrays],
        in_specs=many,
        out_specs=outs,
        scratch_shapes=[pltpu.SemaphoreType.DMA((len(arrays),))],
        name="finish",
    )(*arrays)


def make_stages(n_table, n_rep, parts):
    rep = [("replica", b) for b in range(1, n_rep.bit_length() - 1)]
    tab = [("table", b) for b in range(n_table.bit_length() - 1)]
    bits = rep + tab
    tail = bits[:-1]
    turned = [tail[p % len(tail):] + tail[:p % len(tail)] for p in range(parts)]
    swapped = [p % 3 == 0 for p in range(parts)]
    return [
        part[:-1] + bits[-1:] + part[-1:] if swap else part + bits[-1:]
        for part, swap in zip(turned, swapped)
    ]


def places(stages, n_rep, chips):
    plan = []
    pairs = n_rep // 2
    for part in stages:
        row = []
        for d in range(chips):
            at = 0
            for axis, bit in part:
                number = d // pairs if axis == "table" else (d % pairs) * 2
                at = at * 2 + (number >> bit) % 2
            row.append(at)
        plan.append(row)
    return plan


def fast_local(
    emb_table, cross_up, cross_down, cross_bias, out_weight, bottom_weight, bottom_bias,
    dense_in, labels, lookup_ids, bag_weight, bag_length, want_blocks, hot_blocks, hot_count,
):
    owners, reps = lax.axis_size("table"), lax.axis_size("replica")
    stages = make_stages(owners, reps, PARTS)
    plan = places(stages, reps, owners * reps // 2)
    up, down, table = whole(
        plan, stages, owners, reps, want_blocks.transpose(0, 1, 3, 2), hot_blocks, hot_count, emb_table,
        lookup_ids.transpose(1, 2, 0), bag_weight.transpose(1, 2, 0), bag_length.T,
        dense_in.T, labels[None], cross_up, cross_down, cross_bias, out_weight,
        bottom_weight, bottom_bias[None],
    )
    up, down, table = [pltpu.with_memory_space_constraint(a, pltpu.VMEM) for a in (up, down, table)]
    u, d, t = finish(up, down, table)
    return u, d, t.reshape(-1, EMB)


def local_step(
    cached_rows,
    dense_dev,
    labels_dev,
    ids_dev,
    weight_dev,
    length_dev,
    cross_up,
    cross_down,
    cross_bias,
    out_weight,
    bottom_weight,
    bottom_bias,
):
    batch = ids_dev.shape[0]
    width = cached_rows.shape[1]
    gathered = cached_rows[ids_dev].astype(jnp.float32)
    slots = jnp.arange(ids_dev.shape[2], dtype=jnp.int32)
    bag_coef = jnp.where(
        slots[None, None, :] < length_dev[:, :, None], weight_dev, jnp.zeros((), jnp.float32)
    )
    pooled = jnp.sum(bag_coef[..., None] * gathered, axis=2)
    bottom = jax.nn.relu(
        jnp.dot(dense_dev, bottom_weight, precision=lax.Precision.HIGHEST) + bottom_bias
    )
    cross_base = jnp.concatenate([bottom, pooled.reshape(batch, -1)], 1).astype(jnp.bfloat16)
    low_rank = lax.dot_general(
        cross_base, cross_down, (((1,), (1,)), ((), ())), preferred_element_type=jnp.float32
    ).astype(jnp.bfloat16)
    cross_gate = jnp.dot(low_rank, cross_up, preferred_element_type=jnp.float32) + cross_bias
    base_wide = cross_base.astype(jnp.float32)
    crossed = base_wide * cross_gate + base_wide
    logits = jnp.dot(crossed, out_weight, precision=lax.Precision.HIGHEST)
    logit_grad = jax.nn.sigmoid(logits) - labels_dev.astype(jnp.float32)
    grad_crossed = logit_grad[:, None] * out_weight[None, :]
    g_cross = (grad_crossed * base_wide).astype(jnp.bfloat16)
    g_low = lax.dot_general(
        g_cross, cross_up, (((1,), (1,)), ((), ())), preferred_element_type=jnp.float32
    ).astype(jnp.bfloat16)
    up_part = lax.dot_general(
        low_rank, g_cross, (((0,), (0,)), ((), ())), preferred_element_type=jnp.float32
    )
    down_part = lax.dot_general(
        g_low, cross_base, (((0,), (0,)), ((), ())), preferred_element_type=jnp.float32
    )
    grad_base = grad_crossed * (cross_gate + 1.0) + jnp.dot(
        g_low, cross_down, preferred_element_type=jnp.float32
    )
    grad_pooled = grad_base[:, width:].reshape(batch, -1, width)
    contrib = bag_coef[..., None] * grad_pooled[:, :, None, :]
    cache_grad = (
        jnp.zeros(cached_rows.shape, jnp.float32)
        .at[ids_dev.reshape(-1)]
        .add(contrib.reshape(-1, width))
    )
    return (up_part, down_part, cache_grad)


def plain_local(
    emb_table,
    cross_up,
    cross_down,
    cross_bias,
    out_weight,
    bottom_weight,
    bottom_bias,
    dense_in,
    labels,
    lookup_ids,
    bag_weight,
    bag_length,
    want_blocks,
    hot_blocks,
    hot_count,
):
    owners = lax.axis_size("table")
    blocks = emb_table.reshape(-1, BLOCK, EMB)
    block_total = blocks.shape[0]
    wanted = want_blocks.reshape(owners, want_blocks.shape[3])
    asked_for = lax.all_to_all(wanted, "table", split_axis=0, concat_axis=0, tiled=True)
    flat = emb_table.reshape(block_total, -1)
    numbers = jnp.arange(block_total, dtype=jnp.int32)

    def take(ids):
        pick = (ids.reshape(-1)[:, None] == numbers[None, :]).astype(jnp.bfloat16)
        rows = jnp.dot(pick, flat, preferred_element_type=jnp.float32).astype(jnp.bfloat16)
        return rows.reshape(ids.shape + (BLOCK, EMB))

    served = take(asked_for)
    cold_rows = lax.all_to_all(served, "table", split_axis=0, concat_axis=0, tiled=True)
    slot_count = hot_blocks.shape[1]
    alive = jnp.arange(slot_count, dtype=jnp.int32) < hot_count[0]
    own_hot = jnp.where(alive[:, None, None], take(hot_blocks[0]), jnp.zeros((), jnp.bfloat16))
    hot_rows = lax.all_gather(own_hot[:, None], "table", axis=1, tiled=True)
    cold_count = cold_rows.shape[0] * cold_rows.shape[1] * BLOCK
    cached_rows = jnp.concatenate([cold_rows.reshape(-1, EMB), hot_rows.reshape(-1, EMB)], 0)
    up_part, down_part, cache_grad = local_step(
        cached_rows,
        dense_in,
        labels,
        lookup_ids,
        bag_weight,
        bag_length,
        cross_up,
        cross_down,
        cross_bias,
        out_weight,
        bottom_weight,
        bottom_bias,
    )
    cold_grad = cache_grad[:cold_count].reshape(cold_rows.shape).astype(jnp.bfloat16)
    returned = lax.all_to_all(cold_grad, "table", split_axis=0, concat_axis=0, tiled=True)
    hot_grad = cache_grad[cold_count:].reshape(hot_rows.shape)
    hot_sums = lax.psum_scatter(hot_grad, "table", scatter_dimension=1, tiled=True)[:, 0]
    block_ids = jnp.arange(block_total, dtype=jnp.int32)
    cold_pick = (asked_for.reshape(-1)[:, None] == block_ids[None, :]).astype(jnp.bfloat16)
    hot_pick = ((hot_blocks[0][:, None] == block_ids[None, :]) & alive[:, None]).astype(jnp.float32)
    block_grad = lax.dot_general(
        cold_pick,
        returned.reshape(cold_pick.shape[0], -1),
        (((0,), (0,)), ((), ())),
        preferred_element_type=jnp.float32,
    )
    block_grad = block_grad + lax.dot_general(
        hot_pick,
        hot_sums.reshape(slot_count, -1),
        (((0,), (0,)), ((), ())),
        precision=lax.Precision.HIGHEST,
    )
    table_grad = lax.psum_scatter(
        block_grad.reshape(-1, EMB), "replica", scatter_dimension=0, tiled=True
    )
    up_grad, down_grad = (
        lax.psum_scatter(up_part, ("table", "replica"), scatter_dimension=0, tiled=True),
        lax.psum_scatter(down_part, ("table", "replica"), scatter_dimension=0, tiled=True),
    )
    return (up_grad, down_grad, table_grad)


def choose(mesh, *args):
    devices = mesh.shape["table"] * mesh.shape["replica"]
    powers = all(n > 1 and n & (n - 1) == 0 for n in mesh.shape.values())
    rank, width = args[1].shape
    ids, want, hot = args[9], args[12], args[13]
    cache = mesh.shape["table"] * (want.shape[3] + hot.shape[1]) * BLOCK
    picked = 2 * ids.shape[0] * ids.shape[1] * cache
    whole_tiles = rank % (devices * SUBLANES) == 0 and width % (PARTS * LANES) == 0
    if powers and whole_tiles and ids.shape[0] == LANES and picked < 2**23:
        return fast_local(*args)
    return plain_local(*args)


def solution(mesh):
    local = functools.partial(choose, mesh)
    placed = (
        P("table", None),
        P(),
        P(),
        P(),
        P(),
        P(),
        P(),
        P(("table", "replica"), None),
        P(("table", "replica")),
        P(("table", "replica"), None, None),
        P(("table", "replica"), None, None),
        P(("table", "replica"), None),
        P("table", "replica", None, None),
        P("table", None),
        P("table"),
    )
    return jax.shard_map(
        local,
        mesh=mesh,
        in_specs=placed,
        out_specs=(
            P(("table", "replica"), None),
            P(("table", "replica"), None),
            P(("table", "replica"), None),
        ),
        check_vma=False,
    )
```
